768 devices in a mesh: tile: 96 (over z, y), mode: 8 (over x, core).
Axes of the slice: x: 4, y: 8, z: 12, core: 2. Of those that a mesh axis runs over, the one named last changes fastest.
Arguments:
- intensity: float32 [192, 256, 256], P('tile'), may hold values from 0.05 to 4
- positions: int32 [192, 2], replicated, may hold values from 0 to 24575, as said below
- object_field: float32 [2, 320, 24576], P(None, None, 'tile'), may hold values from -4 to 4
- probe_modes: float32 [8, 2, 256, 256], P('mode'), may hold values from -1.5 to 1.5
- kernel_taps: float32 [2, 129], replicated, may hold values from -0.375 to 0.375
Outputs:
- new_object: float32 [2, 320, 24576], P(None, None, 'tile')
The draws below stay inside these ranges and needn't reach their ends.
Inputs may be any that keep to these rules, and one draw needn't show every extreme that they name: `positions`: pattern g belongs to scan block b = g // 2; its centre column lies in tile b - 1, b or b + 1, tile t holding columns t * 256 to (t + 1) * 256 - 1. From one block at most 1 patterns lie in each neighbouring tile; in every draw some block has 1 in its right neighbour and some block 1 in its left neighbour, and some tile keeps all 2 of its own block and gets 1 from each neighbouring block. Within its tile, the centre column of an even-numbered pattern of a block lies in the last 64 columns, that of an odd-numbered one in the first 64 columns. Rows lie in 0 to 64.
All inputs are finite; a program needn't handle non-finite values.
Results may differ from the reference program's by a relative error of at most 0.0023.
Values sent between devices are 32-bit elements; how exact they have to be, the bound alone decides.
No kernel may reach another device: no remote copies, remote signals or barrier semaphores. Data moves between devices by JAX's collectives and lax.ppermute only.
A program may use at most 32 MiB of HBM per device.

```python
import math
import jax
import jax.numpy as jnp
from jax import lax

P_SIZE = 256
BAND = 64
CAP = 1
SCAN = 2
TW = 256
VRANGE = 64
MODES = 8
HALF = 128
OH = 320
NPAT = 192
NTW = 24576


def draw_positions(key, part):
    blocks = NPAT // SCAN
    key_left, key_right, key_column, key_row = jax.random.split(key, 4)
    block_ids = jnp.arange(blocks, dtype=jnp.int32)
    to_left = jax.random.randint(key_left, (blocks,), 0, CAP + 1, dtype=jnp.int32)
    to_right = jax.random.randint(key_right, (blocks,), 0, CAP + 1, dtype=jnp.int32)
    centre = blocks // 2
    near_centre = (block_ids >= centre - 2) & (block_ids <= centre + 2)
    to_left = jnp.where(near_centre, CAP, to_left)
    to_right = jnp.where(near_centre, CAP, to_right)
    to_left = jnp.where(block_ids == 0, 0, to_left)
    to_right = jnp.where(block_ids == blocks - 1, 0, to_right)
    special = 1
    to_left = jnp.where(block_ids == special, 0, jnp.where(block_ids == special + 1, CAP, to_left))
    to_right = jnp.where(block_ids == special, 0, jnp.where(block_ids == special - 1, CAP, to_right))
    within = jnp.arange(SCAN, dtype=jnp.int32)
    offset = jnp.where(within[None, :] < to_left[:, None], -1, jnp.where(within[None, :] >= SCAN - to_right[:, None], 1, 0))
    owner = block_ids[:, None] + offset
    reach = HALF // 2
    inner_col = jax.random.randint(key_column, (blocks, SCAN), 0, reach, dtype=jnp.int32)
    inner_col = jnp.where(within[None, :] % 2 == 0, TW - reach + inner_col, inner_col)
    columns = owner * TW + inner_col
    top_rows = jax.random.randint(key_row, (blocks, SCAN), 0, VRANGE + 1, dtype=jnp.int32)
    return jnp.stack([top_rows, columns], axis=-1).reshape(NPAT, 2).astype(jnp.int32)


def steps_of(key, shape, shards, least, top_value):
    loudness = 1.0
    for axis_at, blocks in shards:
        heights = jax.random.uniform(jax.random.fold_in(jax.random.fold_in(key, 6), axis_at), (blocks,), jnp.float32, least / len(shards), top_value / len(shards))
        loudness = loudness * jnp.repeat(jnp.exp(heights), shape[axis_at] // blocks).reshape((-1,) + (1,) * (len(shape) - 1 - axis_at))
    return loudness


def bell_draw(stream_key, shape, width, most, shards=(), kind=jnp.bfloat16):
    array = jax.random.normal(stream_key, shape, jnp.float32) * width
    if len(shards) > 0:
        array = steps_of(stream_key, shape, shards, -0.22, 0.18) * array
    return jnp.clip(array, min=-most, max=most).astype(kind)


def setup_inputs(seed: int = 0) -> dict:
    seeds = jax.random.split(jax.random.key(seed), 6)
    intensity = jnp.clip(jnp.exp(math.log(4.0) - 4.3820266 * jax.random.uniform(seeds[0], (NPAT, P_SIZE, P_SIZE), jnp.float32) ** steps_of(seeds[0], (NPAT, P_SIZE, P_SIZE), ((0, 96),), -0.2, 0.2)), 0.05, 4.0)
    positions = draw_positions(jax.random.fold_in(seeds[5], 71), 0)
    object_field = bell_draw(seeds[2], (2, OH, NTW), 0.7, 4.0, ((2, 96),), jnp.float32)
    probe_modes = bell_draw(seeds[3], (MODES, 2, P_SIZE, P_SIZE), 0.25, 1.5, ((0, 8),), jnp.float32)
    kernel_taps = bell_draw(seeds[4], (2, 2 * BAND + 1), (2 * (2 * BAND + 1)) ** -0.5, 0.375, (), jnp.float32)
    return dict(intensity=intensity, positions=positions, object_field=object_field, probe_modes=probe_modes, kernel_taps=kernel_taps)


def band_matrix(taps_row):
    leading = jnp.zeros((P_SIZE - 1 - BAND,), jnp.float32)
    trailing = jnp.zeros((P_SIZE - BAND,), jnp.float32)
    vector = jnp.concatenate([leading, taps_row, trailing])
    tiled = jnp.tile(vector, P_SIZE)[:P_SIZE * (2 * P_SIZE - 1)].reshape(P_SIZE, 2 * P_SIZE - 1)
    return tiled[:, P_SIZE - 1:]

def round_low(values):
    lowered = lax.optimization_barrier(values.astype(jnp.bfloat16))
    return lowered.astype(jnp.float32)

def product(form, left_op, right_op):
    return jnp.einsum(form, left_op.astype(jnp.float32), right_op.astype(jnp.float32))

def forward_pass(wave_re, wave_im, band_re, band_im):
    mid_re = round_low(product('ab,wbc->wac', band_re, wave_re) - product('ab,wbc->wac', band_im, wave_im))
    mid_im = round_low(product('ab,wbc->wac', band_re, wave_im) + product('ab,wbc->wac', band_im, wave_re))
    far_re = product('wab,cb->wac', mid_re, band_re) - product('wab,cb->wac', mid_im, band_im)
    far_im = product('wab,cb->wac', mid_re, band_im) + product('wab,cb->wac', mid_im, band_re)
    return (far_re, far_im)

def backward_pass(near_re, near_im, band_re, band_im):
    mid_re = round_low(product('ba,wbc->wac', band_re, near_re) + product('ba,wbc->wac', band_im, near_im))
    mid_im = round_low(product('ba,wbc->wac', band_re, near_im) - product('ba,wbc->wac', band_im, near_re))
    back_re = product('wab,bc->wac', mid_re, band_re) + product('wab,bc->wac', mid_im, band_im)
    back_im = product('wab,bc->wac', mid_im, band_re) - product('wab,bc->wac', mid_re, band_im)
    return (back_re, back_im)

def reference(intensity, positions, object_field, probe_modes, kernel_taps):
    band_re = round_low(band_matrix(kernel_taps[0]))
    band_im = round_low(band_matrix(kernel_taps[1]))
    padded = jnp.pad(object_field, ((0, 0), (0, 0), (HALF, HALF)))
    probe_re = probe_modes[:, 0]
    probe_im = probe_modes[:, 1]
    anchor = jnp.zeros((), jnp.int32)

    def visit(total, item):
        measured, placed = item
        top_row = placed[0].astype(jnp.int32)
        left_col = placed[1].astype(jnp.int32)
        patch = lax.dynamic_slice(padded, (anchor, top_row, left_col), (2, P_SIZE, P_SIZE))
        exit_re = probe_re * patch[0] - probe_im * patch[1]
        exit_im = probe_re * patch[1] + probe_im * patch[0]
        far_re, far_im = forward_pass(round_low(exit_re), round_low(exit_im), band_re, band_im)
        power = lax.optimization_barrier(jnp.sum(far_re * far_re + far_im * far_im, axis=0))
        ratio = jnp.sqrt(measured) / jnp.sqrt(power + 1.0)
        back_re, back_im = backward_pass(round_low(far_re * ratio), round_low(far_im * ratio), band_re, band_im)
        diff_re = back_re - exit_re
        diff_im = back_im - exit_im
        piece = jnp.stack([lax.optimization_barrier(jnp.sum(probe_re * diff_re + probe_im * diff_im, axis=0)), lax.optimization_barrier(jnp.sum(probe_re * diff_im - probe_im * diff_re, axis=0)), lax.optimization_barrier(jnp.sum(probe_re * probe_re + probe_im * probe_im, axis=0))])
        current = lax.dynamic_slice(total, (anchor, top_row, left_col), (3, P_SIZE, P_SIZE))
        total = lax.dynamic_update_slice(total, current + piece, (anchor, top_row, left_col))
        return (total, None)
    start_total = jnp.zeros((3, OH, NTW + P_SIZE), jnp.float32)
    total, _ = lax.scan(visit, start_total, (intensity, positions))
    inner = total[:, :, HALF:HALF + NTW]
    return object_field + inner[:2] / (inner[2] + 0.5)
```

```python
import functools

import jax
import jax.numpy as jnp
from jax import lax
from jax.experimental import pallas as pl
from jax.experimental.pallas import tpu as pltpu
from jax.sharding import PartitionSpec as P

P_SIZE = 256
BAND = 64
TW = 256
HALF = 128
OH = 320
MODES = 8
EXT = TW + HALF
TALL = P_SIZE + 8
GROUP = 2
F32 = jnp.float32
BF16 = jnp.bfloat16


def place_of(tiles):
    return lax.axis_index("tile"), lax.rem(lax.axis_index("mode"), 2)


def slot_of(pos_ref, tile, core, tiles, shift):
    block = tile + shift
    inside = (block >= 0) & (block < tiles)
    pattern = 2 * jnp.clip(block, 0, tiles - 1) + core
    return inside, pos_ref[0, pattern], pos_ref[1, pattern]


def aligned(top_row):
    extra = lax.rem(top_row, 8)
    return pl.multiple_of(top_row - extra, 8), extra


def lowered(window, extra, width):
    tall = jnp.concatenate([window, jnp.zeros((TALL - P_SIZE, P_SIZE), F32)], axis=0)
    return jnp.concatenate([pltpu.roll(tall, extra, 0), jnp.zeros((TALL, width - P_SIZE), F32)], axis=1)


def pack_kernel(obj, inten, inward, outward, sem):
    core = lax.rem(lax.axis_index("mode"), 2)
    edge = pl.ds(pl.multiple_of(core * HALF, HALF), HALF)
    moves = (
        (obj.at[0, :, edge], inward.at[0:OH]),
        (obj.at[1, :, edge], inward.at[OH : 2 * OH]),
        (inten.at[core, :, 0:HALF], inward.at[2 * OH : 2 * OH + P_SIZE]),
        (inten.at[core, :, HALF:P_SIZE], inward.at[2 * OH + P_SIZE : 2 * OH + 2 * P_SIZE]),
        (inten.at[core], outward),
    )
    copies = [pltpu.make_async_copy(src, dst, sem.at[i]) for i, (src, dst) in enumerate(moves)]
    for copy in copies:
        copy.start()
    for copy in copies:
        copy.wait()


def main_kernel(tiles, pos_ref, taps_ref, int_own, inward, outward, obj, *rest):
    probes_in = rest[:MODES]
    mid_out, rim_out, weight_out = rest[MODES : MODES + 3]
    (wave, total, meas, probe, far, low, midb, stack, stack_t, ratio, patch, acc, row_pad, sem) = rest[MODES + 3 :]
    tile, core = place_of(tiles)

    copies = []

    def bring(src, dst):
        copy = pltpu.make_async_copy(src, dst, sem.at[len(copies)])
        copy.start()
        copies.append(copy)

    rim = pl.ds(pl.multiple_of((1 - core) * TW, HALF), HALF)
    bring(obj, wave.at[:, :OH, pl.ds(pl.multiple_of(core * HALF, HALF), TW)])
    bring(inward.at[0:OH], wave.at[0, :OH, rim])
    bring(inward.at[OH : 2 * OH], wave.at[1, :OH, rim])
    bring(outward, meas.at[0])
    bring(int_own.at[core], meas.at[1])
    bring(inward.at[2 * OH : 2 * OH + P_SIZE], meas.at[2, :, 0:HALF])
    bring(inward.at[2 * OH + P_SIZE : 2 * OH + 2 * P_SIZE], meas.at[2, :, HALF:P_SIZE])
    for index in range(MODES):
        bring(probes_in[index].at[0], probe.at[index])

    row_pad[...] = jnp.zeros_like(row_pad)
    row_pad[0:2, 0 : 2 * BAND + 1] = taps_ref[...]

    def band(part):
        line = jnp.broadcast_to(row_pad[part : part + 1, :], (P_SIZE, 2 * P_SIZE))
        turned = pltpu.roll(line, 2 * P_SIZE - BAND, 1, stride=1, stride_axis=0)
        return turned[:, :P_SIZE]

    band_re = band(0)
    band_im = band(1)
    stack[:P_SIZE, :P_SIZE] = band_re.astype(BF16)
    stack[:P_SIZE, P_SIZE:] = (-band_im).astype(BF16)
    stack[P_SIZE:, :P_SIZE] = band_im.astype(BF16)
    stack[P_SIZE:, P_SIZE:] = band_re.astype(BF16)
    turned_re = band_re.T
    turned_im = band_im.T
    stack_t[:P_SIZE, :P_SIZE] = turned_re.astype(BF16)
    stack_t[:P_SIZE, P_SIZE:] = turned_im.astype(BF16)
    stack_t[P_SIZE:, :P_SIZE] = (-turned_im).astype(BF16)
    stack_t[P_SIZE:, P_SIZE:] = turned_re.astype(BF16)

    total[...] = jnp.zeros_like(total)
    for copy in copies:
        copy.wait()

    weight_out[...] = jnp.zeros_like(weight_out)

    @pl.loop(0, MODES)
    def _(mode):
        weight_out[...] += probe[mode, 0] * probe[mode, 0] + probe[mode, 1] * probe[mode, 1]

    def mix(first, second):
        mid = jnp.dot(first[...], low[...], preferred_element_type=F32)
        for unit in range(GROUP):
            own = slice(unit * P_SIZE, (unit + 1) * P_SIZE)
            midb[own, :P_SIZE] = mid[:P_SIZE, own].astype(BF16)
            midb[own, P_SIZE:] = mid[P_SIZE:, own].astype(BF16)
        return jnp.dot(midb[...], second[...], preferred_element_type=F32)

    @pl.loop(0, 3)
    def _(slot):
        shift = (slot - 1) * (1 - 2 * core)
        inside, top_row, column = slot_of(pos_ref, tile, core, tiles, shift)
        offset = column - tile * TW - (1 - core) * HALF
        here = inside & (column >= tile * TW) & (column < (tile + 1) * TW)

        @pl.when(here)
        def _():
            base, extra = aligned(top_row)
            for part in range(2):
                rows = wave[part, pl.ds(base, TALL), :]
                turned = pltpu.roll(rows, lax.rem(EXT - offset, EXT), 1)[:, :P_SIZE]
                patch[part] = pltpu.roll(turned, lax.rem(TALL - extra, TALL), 0)[:P_SIZE]
            for start in range(0, MODES, GROUP):
                for unit in range(GROUP):
                    own = slice(unit * P_SIZE, (unit + 1) * P_SIZE)
                    pr = probe[start + unit, 0]
                    pi = probe[start + unit, 1]
                    low[:P_SIZE, own] = (pr * patch[0] - pi * patch[1]).astype(BF16)
                    low[P_SIZE:, own] = (pr * patch[1] + pi * patch[0]).astype(BF16)
                out = mix(stack, stack_t)
                power = 0.0
                for unit in range(GROUP):
                    block = out[unit * P_SIZE : (unit + 1) * P_SIZE]
                    far[start + unit] = block
                    power += block[:, :P_SIZE] * block[:, :P_SIZE] + block[:, P_SIZE:] * block[:, P_SIZE:]
                ratio[...] = power if start == 0 else ratio[...] + power

            ratio[...] = jnp.sqrt(meas[slot]) / jnp.sqrt(ratio[...] + 1.0)
            acc[0] = -weight_out[...] * patch[0]
            acc[1] = -weight_out[...] * patch[1]

            for start in range(0, MODES, GROUP):
                for unit in range(GROUP):
                    own = slice(unit * P_SIZE, (unit + 1) * P_SIZE)
                    low[:P_SIZE, own] = (far[start + unit, :, :P_SIZE] * ratio[...]).astype(BF16)
                    low[P_SIZE:, own] = (far[start + unit, :, P_SIZE:] * ratio[...]).astype(BF16)
                out = mix(stack_t, stack)
                term_re = 0.0
                term_im = 0.0
                for unit in range(GROUP):
                    back_re = out[unit * P_SIZE : (unit + 1) * P_SIZE, :P_SIZE]
                    back_im = out[unit * P_SIZE : (unit + 1) * P_SIZE, P_SIZE:]
                    pr = probe[start + unit, 0]
                    pi = probe[start + unit, 1]
                    term_re += pr * back_re + pi * back_im
                    term_im += pr * back_im - pi * back_re
                acc[0] += term_re
                acc[1] += term_im

            for part in range(2):
                total[part, pl.ds(base, TALL), :] += pltpu.roll(lowered(acc[part], extra, EXT), offset, 1)

    mid_out[...] = total[:, :OH, pl.ds(pl.multiple_of(core * HALF, HALF), TW)]
    rim_out[...] = total[:, :OH, rim]


def denom_kernel(tiles, pos_ref, weight_in, scale, denom, weight, sem):
    tile, _ = place_of(tiles)
    copy = pltpu.make_async_copy(weight_in, weight, sem)
    copy.start()
    copy.wait()
    denom[...] = jnp.zeros_like(denom)
    for parity, shifts in ((0, (-2, -1, 0, 1)), (1, (-1, 0, 1, 2))):
        for shift in shifts:
            inside, top_row, column = slot_of(pos_ref, tile, parity, tiles, shift)
            start = column - HALF - tile * TW

            @pl.when(inside & (start > -P_SIZE) & (start < TW))
            def _():
                base, extra = aligned(top_row)
                wide = lowered(weight[...], extra, 2 * P_SIZE)
                turned = pltpu.roll(wide, jnp.where(start < 0, start + 2 * P_SIZE, start), 1)
                denom[pl.ds(base, TALL), :] += turned[:, :TW]

    scale[...] = 1.0 / (denom[:OH] + 0.5)


ANY = pl.BlockSpec(memory_space=pl.ANY)
VMEM = pl.BlockSpec(memory_space=pltpu.VMEM)
SMEM = pl.BlockSpec(memory_space=pltpu.SMEM)


def local(intensity, positions, object_field, probe_modes, kernel_taps):
    tiles = lax.axis_size("tile")
    modes = lax.axis_size("mode")
    core = lax.rem(lax.axis_index("mode"), 2)
    spots = positions.T

    def along_x(array, steps):
        return lax.ppermute(array, "mode", [(i, (i + 2 * steps) % modes) for i in range(modes)])

    def swap(array):
        return lax.ppermute(array, "mode", [(i, i ^ 1) for i in range(modes)])

    def between_tiles(array, cross):
        pairs = []
        for tile in range(tiles):
            for mode in range(modes):
                target = tile + 1 if mode % 2 == 0 else tile - 1
                if 0 <= target < tiles:
                    pairs.append((tile * modes + mode, target * modes + (mode ^ 1 if cross else mode)))
        return lax.ppermute(array, ("tile", "mode"), pairs)

    def from_tile(array, step):
        pairs = []
        for tile in range(tiles):
            for mode in range(modes):
                source = tile + step if mode % 2 == 0 else tile - step
                if 0 <= source < tiles:
                    pairs.append((source * modes + mode, tile * modes + mode))
        return lax.ppermute(array, ("tile", "mode"), pairs)

    ring = [along_x(probe_modes, step) for step in (1, -1, 2)]
    inward, outward = pl.pallas_call(
        pack_kernel,
        out_shape=(
            jax.ShapeDtypeStruct((2 * OH + 2 * P_SIZE, HALF), F32),
            jax.ShapeDtypeStruct((P_SIZE, P_SIZE), F32),
        ),
        in_specs=[ANY, ANY],
        out_specs=(ANY, ANY),
        scratch_shapes=[pltpu.SemaphoreType.DMA((5,))],
        name="pack",
    )(object_field, intensity)
    inward = from_tile(inward, 1)
    outward = from_tile(outward, -1)
    ring[0], ring[1], inward, outward = lax.optimization_barrier((ring[0], ring[1], inward, outward))
    own = [probe_modes] + ring
    probes = own + [swap(array) for array in own]

    middle, rim, weight = pl.pallas_call(
        functools.partial(main_kernel, tiles),
        out_shape=(
            jax.ShapeDtypeStruct((2, OH, TW), F32),
            jax.ShapeDtypeStruct((2, OH, HALF), F32),
            jax.ShapeDtypeStruct((P_SIZE, P_SIZE), F32),
        ),
        in_specs=[SMEM, VMEM] + [ANY] * (4 + MODES),
        out_specs=(VMEM, VMEM, VMEM),
        scratch_shapes=[
            pltpu.VMEM((2, OH + 8, EXT), F32),
            pltpu.VMEM((2, OH + 8, EXT), F32),
            pltpu.VMEM((3, P_SIZE, P_SIZE), F32),
            pltpu.VMEM((MODES, 2, P_SIZE, P_SIZE), F32),
            pltpu.VMEM((MODES, P_SIZE, 2 * P_SIZE), F32),
            pltpu.VMEM((2 * P_SIZE, GROUP * P_SIZE), BF16),
            pltpu.VMEM((GROUP * P_SIZE, 2 * P_SIZE), BF16),
            pltpu.VMEM((2 * P_SIZE, 2 * P_SIZE), BF16),
            pltpu.VMEM((2 * P_SIZE, 2 * P_SIZE), BF16),
            pltpu.VMEM((P_SIZE, P_SIZE), F32),
            pltpu.VMEM((2, P_SIZE, P_SIZE), F32),
            pltpu.VMEM((2, P_SIZE, P_SIZE), F32),
            pltpu.VMEM((8, 2 * P_SIZE), F32),
            pltpu.SemaphoreType.DMA((7 + MODES,)),
        ],
        compiler_params=pltpu.CompilerParams(vmem_limit_bytes=28 * 2**20),
        name="update_terms",
    )(spots, kernel_taps, intensity, inward, outward, object_field, *probes)

    rim_same = between_tiles(rim, False)
    rim_cross = between_tiles(rim, True)
    scale = pl.pallas_call(
        functools.partial(denom_kernel, tiles),
        out_shape=jax.ShapeDtypeStruct((OH, TW), F32),
        in_specs=[SMEM, ANY],
        out_specs=VMEM,
        scratch_shapes=[
            pltpu.VMEM((OH + 8, TW), F32),
            pltpu.VMEM((P_SIZE, P_SIZE), F32),
            pltpu.SemaphoreType.DMA,
        ],
        name="denominator",
    )(spots, weight)
    other = swap(middle)
    low = jnp.where(core == 0, rim_same, rim_cross)
    high = jnp.where(core == 0, rim_cross, rim_same)
    return object_field + (middle + other + jnp.concatenate([low, high], axis=2)) * scale


def solution(mesh):
    return jax.shard_map(
        local,
        mesh=mesh,
        in_specs=(
            P("tile", None, None),
            P(),
            P(None, None, "tile"),
            P("mode", None, None, None),
            P(),
        ),
        out_specs=P(None, None, "tile"),
        check_vma=False,
    )
```

```python
import functools

import jax
import jax.numpy as jnp
from jax import lax
from jax.experimental import pallas as pl
from jax.experimental.pallas import tpu as pltpu
from jax.sharding import PartitionSpec as P

P_SIZE = 256
BAND = 64
TW = 256
HALF = 128
OH = 320
MODES = 8
EXT = TW + HALF
TALL = P_SIZE + 8
GROUP = 2
F32 = jnp.float32
BF16 = jnp.bfloat16


def place_of(tiles):
    return lax.axis_index("tile"), lax.rem(lax.axis_index("mode"), 2)


def slot_of(pos_ref, tile, core, tiles, shift):
    block = tile + shift
    inside = (block >= 0) & (block < tiles)
    pattern = 2 * jnp.clip(block, 0, tiles - 1) + core
    return inside, pos_ref[0, pattern], pos_ref[1, pattern]


def aligned(top_row):
    extra = lax.rem(top_row, 8)
    return pl.multiple_of(top_row - extra, 8), extra


def lowered(window, extra, width):
    tall = jnp.concatenate([window, jnp.zeros((TALL - P_SIZE, P_SIZE), F32)], axis=0)
    return jnp.concatenate([pltpu.roll(tall, extra, 0), jnp.zeros((TALL, width - P_SIZE), F32)], axis=1)


def pack_kernel(obj, inten, inward, outward, sem):
    core = lax.rem(lax.axis_index("mode"), 2)
    edge = pl.ds(pl.multiple_of(core * HALF, HALF), HALF)
    moves = (
        (obj.at[0, :, edge], inward.at[0:OH]),
        (obj.at[1, :, edge], inward.at[OH : 2 * OH]),
        (inten.at[core, :, 0:HALF], inward.at[2 * OH : 2 * OH + P_SIZE]),
        (inten.at[core, :, HALF:P_SIZE], inward.at[2 * OH + P_SIZE : 2 * OH + 2 * P_SIZE]),
        (inten.at[core], outward),
    )
    copies = [pltpu.make_async_copy(src, dst, sem.at[i]) for i, (src, dst) in enumerate(moves)]
    for copy in copies:
        copy.start()
    for copy in copies:
        copy.wait()


def main_kernel(tiles, pos_ref, taps_ref, int_own, inward, outward, obj, *rest):
    probes_in = rest[:MODES]
    mid_out, rim_out, weight_out = rest[MODES : MODES + 3]
    (wave, total, meas, probe, far, low, midb, stack, stack_t, ratio, patch, acc, row_pad, sem) = rest[MODES + 3 :]
    tile, core = place_of(tiles)

    copies = []

    def bring(src, dst):
        copy = pltpu.make_async_copy(src, dst, sem.at[len(copies)])
        copy.start()
        copies.append(copy)

    rim = pl.ds(pl.multiple_of((1 - core) * TW, HALF), HALF)
    bring(obj, wave.at[:, :OH, pl.ds(pl.multiple_of(core * HALF, HALF), TW)])
    bring(inward.at[0:OH], wave.at[0, :OH, rim])
    bring(inward.at[OH : 2 * OH], wave.at[1, :OH, rim])
    bring(outward, meas.at[0])
    bring(int_own.at[core], meas.at[1])
    bring(inward.at[2 * OH : 2 * OH + P_SIZE], meas.at[2, :, 0:HALF])
    bring(inward.at[2 * OH + P_SIZE : 2 * OH + 2 * P_SIZE], meas.at[2, :, HALF:P_SIZE])
    for index in range(MODES):
        bring(probes_in[index].at[0], probe.at[index])

    row_pad[...] = jnp.zeros_like(row_pad)
    row_pad[0:2, 0 : 2 * BAND + 1] = taps_ref[...]

    def band(part):
        line = jnp.broadcast_to(row_pad[part : part + 1, :], (P_SIZE, 2 * P_SIZE))
        turned = pltpu.roll(line, 2 * P_SIZE - BAND, 1, stride=1, stride_axis=0)
        return turned[:, :P_SIZE]

    band_re = band(0)
    band_im = band(1)
    stack[:P_SIZE, :P_SIZE] = band_re.astype(BF16)
    stack[:P_SIZE, P_SIZE:] = (-band_im).astype(BF16)
    stack[P_SIZE:, :P_SIZE] = band_im.astype(BF16)
    stack[P_SIZE:, P_SIZE:] = band_re.astype(BF16)
    turned_re = band_re.T
    turned_im = band_im.T
    stack_t[:P_SIZE, :P_SIZE] = turned_re.astype(BF16)
    stack_t[:P_SIZE, P_SIZE:] = turned_im.astype(BF16)
    stack_t[P_SIZE:, :P_SIZE] = (-turned_im).astype(BF16)
    stack_t[P_SIZE:, P_SIZE:] = turned_re.astype(BF16)

    total[...] = jnp.zeros_like(total)
    for copy in copies:
        copy.wait()

    weight_out[...] = jnp.zeros_like(weight_out)

    @pl.loop(0, MODES)
    def _(mode):
        weight_out[...] += probe[mode, 0] * probe[mode, 0] + probe[mode, 1] * probe[mode, 1]

    def mix(first, second):
        mid = jnp.dot(first[...], low[...], preferred_element_type=F32)
        for unit in range(GROUP):
            own = slice(unit * P_SIZE, (unit + 1) * P_SIZE)
            midb[own, :P_SIZE] = mid[:P_SIZE, own].astype(BF16)
            midb[own, P_SIZE:] = mid[P_SIZE:, own].astype(BF16)
        return jnp.dot(midb[...], second[...], preferred_element_type=F32)

    @pl.loop(0, 3)
    def _(slot):
        shift = (slot - 1) * (1 - 2 * core)
        inside, top_row, column = slot_of(pos_ref, tile, core, tiles, shift)
        offset = column - tile * TW - (1 - core) * HALF
        here = inside & (column >= tile * TW) & (column < (tile + 1) * TW)

        @pl.when(here)
        def _():
            base, extra = aligned(top_row)
            for part in range(2):
                rows = wave[part, pl.ds(base, TALL), :]
                turned = pltpu.roll(rows, lax.rem(EXT - offset, EXT), 1)[:, :P_SIZE]
                patch[part] = pltpu.roll(turned, lax.rem(TALL - extra, TALL), 0)[:P_SIZE]
            for start in range(0, MODES, GROUP):
                for unit in range(GROUP):
                    own = slice(unit * P_SIZE, (unit + 1) * P_SIZE)
                    pr = probe[start + unit, 0]
                    pi = probe[start + unit, 1]
                    low[:P_SIZE, own] = (pr * patch[0] - pi * patch[1]).astype(BF16)
                    low[P_SIZE:, own] = (pr * patch[1] + pi * patch[0]).astype(BF16)
                out = mix(stack, stack_t)
                power = 0.0
                for unit in range(GROUP):
                    block = out[unit * P_SIZE : (unit + 1) * P_SIZE]
                    far[start + unit] = block
                    power += block[:, :P_SIZE] * block[:, :P_SIZE] + block[:, P_SIZE:] * block[:, P_SIZE:]
                ratio[...] = power if start == 0 else ratio[...] + power

            ratio[...] = jnp.sqrt(meas[slot]) / jnp.sqrt(ratio[...] + 1.0)
            acc[0] = -weight_out[...] * patch[0]
            acc[1] = -weight_out[...] * patch[1]

            for start in range(0, MODES, GROUP):
                for unit in range(GROUP):
                    own = slice(unit * P_SIZE, (unit + 1) * P_SIZE)
                    low[:P_SIZE, own] = (far[start + unit, :, :P_SIZE] * ratio[...]).astype(BF16)
                    low[P_SIZE:, own] = (far[start + unit, :, P_SIZE:] * ratio[...]).astype(BF16)
                out = mix(stack_t, stack)
                term_re = 0.0
                term_im = 0.0
                for unit in range(GROUP):
                    back_re = out[unit * P_SIZE : (unit + 1) * P_SIZE, :P_SIZE]
                    back_im = out[unit * P_SIZE : (unit + 1) * P_SIZE, P_SIZE:]
                    pr = probe[start + unit, 0]
                    pi = probe[start + unit, 1]
                    term_re += pr * back_re + pi * back_im
                    term_im += pr * back_im - pi * back_re
                acc[0] += term_re
                acc[1] += term_im

            for part in range(2):
                total[part, pl.ds(base, TALL), :] += pltpu.roll(lowered(acc[part], extra, EXT), offset, 1)

    mid_out[...] = total[:, :OH, pl.ds(pl.multiple_of(core * HALF, HALF), TW)]
    rim_out[...] = total[:, :OH, rim]


def denom_kernel(tiles, pos_ref, weight_in, scale, denom, weight, sem):
    tile, _ = place_of(tiles)
    copy = pltpu.make_async_copy(weight_in, weight, sem)
    copy.start()
    copy.wait()
    denom[...] = jnp.zeros_like(denom)
    for parity, shifts in ((0, (-2, -1, 0, 1)), (1, (-1, 0, 1, 2))):
        for shift in shifts:
            inside, top_row, column = slot_of(pos_ref, tile, parity, tiles, shift)
            start = column - HALF - tile * TW

            @pl.when(inside & (start > -P_SIZE) & (start < TW))
            def _():
                base, extra = aligned(top_row)
                wide = lowered(weight[...], extra, 2 * P_SIZE)
                turned = pltpu.roll(wide, jnp.where(start < 0, start + 2 * P_SIZE, start), 1)
                denom[pl.ds(base, TALL), :] += turned[:, :TW]

    scale[...] = 1.0 / (denom[:OH] + 0.5)


ANY = pl.BlockSpec(memory_space=pl.ANY)
VMEM = pl.BlockSpec(memory_space=pltpu.VMEM)
SMEM = pl.BlockSpec(memory_space=pltpu.SMEM)


def local(intensity, positions, object_field, probe_modes, kernel_taps):
    tiles = lax.axis_size("tile")
    modes = lax.axis_size("mode")
    core = lax.rem(lax.axis_index("mode"), 2)
    spots = positions.T

    def along_x(array, steps):
        return lax.ppermute(array, "mode", [(i, (i + 2 * steps) % modes) for i in range(modes)])

    def swap(array):
        return lax.ppermute(array, "mode", [(i, i ^ 1) for i in range(modes)])

    def between_tiles(array, cross):
        pairs = []
        for tile in range(tiles):
            for mode in range(modes):
                target = tile + 1 if mode % 2 == 0 else tile - 1
                if 0 <= target < tiles:
                    pairs.append((tile * modes + mode, target * modes + (mode ^ 1 if cross else mode)))
        return lax.ppermute(array, ("tile", "mode"), pairs)

    def from_tile(array, step):
        pairs = []
        for tile in range(tiles):
            for mode in range(modes):
                source = tile + step if mode % 2 == 0 else tile - step
                if 0 <= source < tiles:
                    pairs.append((source * modes + mode, tile * modes + mode))
        return lax.ppermute(array, ("tile", "mode"), pairs)

    ring = [along_x(probe_modes, step) for step in (1, -1, 2)]
    inward, outward = pl.pallas_call(
        pack_kernel,
        out_shape=(
            jax.ShapeDtypeStruct((2 * OH + 2 * P_SIZE, HALF), F32),
            jax.ShapeDtypeStruct((P_SIZE, P_SIZE), F32),
        ),
        in_specs=[ANY, ANY],
        out_specs=(VMEM, VMEM),
        scratch_shapes=[pltpu.SemaphoreType.DMA((5,))],
        name="pack",
    )(object_field, intensity)
    inward = from_tile(inward, 1)
    outward = from_tile(outward, -1)
    ring[0], ring[1], inward, outward = lax.optimization_barrier((ring[0], ring[1], inward, outward))
    own = [probe_modes] + ring
    probes = own + [swap(array) for array in own]

    middle, rim, weight = pl.pallas_call(
        functools.partial(main_kernel, tiles),
        out_shape=(
            jax.ShapeDtypeStruct((2, OH, TW), F32),
            jax.ShapeDtypeStruct((2, OH, HALF), F32),
            jax.ShapeDtypeStruct((P_SIZE, P_SIZE), F32),
        ),
        in_specs=[SMEM, VMEM] + [ANY] * (4 + MODES),
        out_specs=(VMEM, VMEM, VMEM),
        scratch_shapes=[
            pltpu.VMEM((2, OH + 8, EXT), F32),
            pltpu.VMEM((2, OH + 8, EXT), F32),
            pltpu.VMEM((3, P_SIZE, P_SIZE), F32),
            pltpu.VMEM((MODES, 2, P_SIZE, P_SIZE), F32),
            pltpu.VMEM((MODES, P_SIZE, 2 * P_SIZE), F32),
            pltpu.VMEM((2 * P_SIZE, GROUP * P_SIZE), BF16),
            pltpu.VMEM((GROUP * P_SIZE, 2 * P_SIZE), BF16),
            pltpu.VMEM((2 * P_SIZE, 2 * P_SIZE), BF16),
            pltpu.VMEM((2 * P_SIZE, 2 * P_SIZE), BF16),
            pltpu.VMEM((P_SIZE, P_SIZE), F32),
            pltpu.VMEM((2, P_SIZE, P_SIZE), F32),
            pltpu.VMEM((2, P_SIZE, P_SIZE), F32),
            pltpu.VMEM((8, 2 * P_SIZE), F32),
            pltpu.SemaphoreType.DMA((7 + MODES,)),
        ],
        compiler_params=pltpu.CompilerParams(vmem_limit_bytes=28 * 2**20),
        name="update_terms",
    )(spots, kernel_taps, intensity, inward, outward, object_field, *probes)

    rim_same = between_tiles(rim, False)
    rim_cross = between_tiles(rim, True)
    scale = pl.pallas_call(
        functools.partial(denom_kernel, tiles),
        out_shape=jax.ShapeDtypeStruct((OH, TW), F32),
        in_specs=[SMEM, ANY],
        out_specs=VMEM,
        scratch_shapes=[
            pltpu.VMEM((OH + 8, TW), F32),
            pltpu.VMEM((P_SIZE, P_SIZE), F32),
            pltpu.SemaphoreType.DMA,
        ],
        name="denominator",
    )(spots, weight)
    other = swap(middle)
    low = jnp.where(core == 0, rim_same, rim_cross)
    high = jnp.where(core == 0, rim_cross, rim_same)
    return object_field + (middle + other + jnp.concatenate([low, high], axis=2)) * scale


def solution(mesh):
    return jax.shard_map(
        local,
        mesh=mesh,
        in_specs=(
            P("tile", None, None),
            P(),
            P(None, None, "tile"),
            P("mode", None, None, None),
            P(),
        ),
        out_specs=P(None, None, "tile"),
        check_vma=False,
    )
```

```python
import functools

import jax
import jax.numpy as jnp
from jax import lax
from jax.experimental import pallas as pl
from jax.experimental.pallas import tpu as pltpu
from jax.sharding import PartitionSpec as P

P_SIZE = 256
BAND = 64
TW = 256
HALF = 128
OH = 320
MODES = 8
EXT = TW + HALF
TALL = P_SIZE + 8
GROUP = 2
HELD = MODES // 2
F32 = jnp.float32
BF16 = jnp.bfloat16


def place_of(tiles):
    return lax.axis_index("tile"), lax.rem(lax.axis_index("mode"), 2)


def slot_of(pos_ref, tile, core, tiles, shift):
    block = tile + shift
    inside = (block >= 0) & (block < tiles)
    pattern = 2 * jnp.clip(block, 0, tiles - 1) + core
    return inside, pos_ref[0, pattern], pos_ref[1, pattern]


def aligned(top_row):
    extra = lax.rem(top_row, 8)
    return pl.multiple_of(top_row - extra, 8), extra


def lowered(window, extra, width):
    tall = jnp.concatenate([window, jnp.zeros((TALL - P_SIZE, P_SIZE), F32)], axis=0)
    return jnp.concatenate([pltpu.roll(tall, extra, 0), jnp.zeros((TALL, width - P_SIZE), F32)], axis=1)


def pack_kernel(obj, inten, halo, chosen, sem):
    core = lax.rem(lax.axis_index("mode"), 2)
    edge = pl.ds(pl.multiple_of(core * HALF, HALF), HALF)
    run_copies([(obj.at[:, :, edge], halo), (inten.at[core], chosen)], sem)


def run_copies(moves, sem):
    copies = [pltpu.make_async_copy(src, dst, sem.at[i]) for i, (src, dst) in enumerate(moves)]
    for copy in copies:
        copy.start()
    for copy in copies:
        copy.wait()


def merge_kernel(own, first, second, third, merged, sem):
    arrays = (own, first, second, third)
    run_copies([(array.at[0], merged.at[2 * i : 2 * i + 2]) for i, array in enumerate(arrays)], sem)


def window_of(pos_ref, tiles, slot):
    tile, core = place_of(tiles)
    inside, top_row, column = slot_of(pos_ref, tile, core, tiles, (slot - 1) * (1 - 2 * core))
    offset = column - tile * TW - (1 - core) * HALF
    here = inside & (column >= tile * TW) & (column < (tile + 1) * TW)
    return here, top_row, offset


def mix(first, second, low, midb):
    mid = jnp.dot(first, low[...], preferred_element_type=F32)
    for unit in range(GROUP):
        own = slice(unit * P_SIZE, (unit + 1) * P_SIZE)
        midb[own, :P_SIZE] = mid[:P_SIZE, own].astype(BF16)
        midb[own, P_SIZE:] = mid[P_SIZE:, own].astype(BF16)
    return jnp.dot(midb[...], second, preferred_element_type=F32)


def forward(probe, patch_re, patch_im, stacks, low, midb, far, power):
    for start in range(0, HELD, GROUP):
        for unit in range(GROUP):
            own = slice(unit * P_SIZE, (unit + 1) * P_SIZE)
            pr = probe[2 * (start + unit)]
            pi = probe[2 * (start + unit) + 1]
            low[:P_SIZE, own] = (pr * patch_re[...] - pi * patch_im[...]).astype(BF16)
            low[P_SIZE:, own] = (pr * patch_im[...] + pi * patch_re[...]).astype(BF16)
        out = mix(stacks[0], stacks[1], low, midb)
        for unit in range(GROUP):
            block = out[unit * P_SIZE : (unit + 1) * P_SIZE]
            far[start + unit] = block
            term = block[:, :P_SIZE] * block[:, :P_SIZE] + block[:, P_SIZE:] * block[:, P_SIZE:]
            power[...] += term


def first_kernel(tiles, pos_ref, taps_ref, obj, halo, mine, far, patch, power, stacks, wave, low, midb, row_pad, sem):
    _, core = place_of(tiles)
    rim = pl.ds(pl.multiple_of((1 - core) * TW, HALF), HALF)
    moves = (
        (obj, wave.at[:, :OH, pl.ds(pl.multiple_of(core * HALF, HALF), TW)]),
        (halo, wave.at[:, :OH, rim]),
    )
    copies = [pltpu.make_async_copy(src, dst, sem.at[i]) for i, (src, dst) in enumerate(moves)]
    for copy in copies:
        copy.start()

    row_pad[...] = jnp.zeros_like(row_pad)
    row_pad[0:2, 0 : 2 * BAND + 1] = taps_ref[...]

    def band(part):
        line = jnp.broadcast_to(row_pad[part : part + 1, :], (P_SIZE, 2 * P_SIZE))
        turned = pltpu.roll(line, 2 * P_SIZE - BAND, 1, stride=1, stride_axis=0)
        return turned[:, :P_SIZE]

    band_re = band(0)
    band_im = band(1)
    turned_re = band_re.T
    turned_im = band_im.T
    for which, blocks in enumerate(((band_re, -band_im, band_im), (turned_re, turned_im, -turned_im))):
        stacks[which, :P_SIZE, :P_SIZE] = blocks[0].astype(BF16)
        stacks[which, :P_SIZE, P_SIZE:] = blocks[1].astype(BF16)
        stacks[which, P_SIZE:, :P_SIZE] = blocks[2].astype(BF16)
        stacks[which, P_SIZE:, P_SIZE:] = blocks[0].astype(BF16)

    for copy in copies:
        copy.wait()

    @pl.loop(0, 3)
    def _(slot):
        here, top_row, offset = window_of(pos_ref, tiles, slot)

        @pl.when(here)
        def _():
            base, extra = aligned(top_row)
            for part in range(2):
                rows = wave[part, pl.ds(base, TALL), :]
                turned = pltpu.roll(rows, lax.rem(EXT - offset, EXT), 1)[:, :P_SIZE]
                patch[slot, part] = pltpu.roll(turned, lax.rem(TALL - extra, TALL), 0)[:P_SIZE]
            power[slot] = jnp.zeros((P_SIZE, P_SIZE), F32)
            forward(mine, patch.at[slot, 0], patch.at[slot, 1], stacks, low, midb, far.at[slot], power.at[slot])


def second_kernel(
    tiles, pos_ref, inten, inward, outward, mine, theirs, far, patch, power, stacks, mid_out, rim_out, weight,
    total, meas, far_too, low, midb, ratio, acc,
):
    _, core = place_of(tiles)
    total[...] = jnp.zeros_like(total)
    meas[0] = outward[...]
    meas[1] = inten[core]
    meas[2] = inward[...]
    weight[...] = jnp.zeros_like(weight)

    @pl.loop(0, MODES)
    def _(plane):
        weight[...] += mine[plane] * mine[plane] + theirs[plane] * theirs[plane]

    @pl.loop(0, 3)
    def _(slot):
        here, top_row, offset = window_of(pos_ref, tiles, slot)

        @pl.when(here)
        def _():
            base, extra = aligned(top_row)
            ratio[...] = power[slot]
            forward(theirs, patch.at[slot, 0], patch.at[slot, 1], stacks, low, midb, far_too, ratio)
            ratio[...] = jnp.sqrt(meas[slot]) / jnp.sqrt(ratio[...] + 1.0)
            acc[0] = -weight[...] * patch[slot, 0]
            acc[1] = -weight[...] * patch[slot, 1]
            for source, probe in ((far.at[slot], mine), (far_too, theirs)):
                for start in range(0, HELD, GROUP):
                    for unit in range(GROUP):
                        own = slice(unit * P_SIZE, (unit + 1) * P_SIZE)
                        low[:P_SIZE, own] = (source[start + unit, :, :P_SIZE] * ratio[...]).astype(BF16)
                        low[P_SIZE:, own] = (source[start + unit, :, P_SIZE:] * ratio[...]).astype(BF16)
                    out = mix(stacks[1], stacks[0], low, midb)
                    term_re = 0.0
                    term_im = 0.0
                    for unit in range(GROUP):
                        back_re = out[unit * P_SIZE : (unit + 1) * P_SIZE, :P_SIZE]
                        back_im = out[unit * P_SIZE : (unit + 1) * P_SIZE, P_SIZE:]
                        pr = probe[2 * (start + unit)]
                        pi = probe[2 * (start + unit) + 1]
                        term_re += pr * back_re + pi * back_im
                        term_im += pr * back_im - pi * back_re
                    acc[0] += term_re
                    acc[1] += term_im

            for part in range(2):
                total[part, pl.ds(base, TALL), :] += pltpu.roll(lowered(acc[part], extra, EXT), offset, 1)

    mid_out[...] = total[:, :OH, pl.ds(pl.multiple_of(core * HALF, HALF), TW)]
    rim_out[...] = total[:, :OH, pl.ds(pl.multiple_of((1 - core) * TW, HALF), HALF)]


def denom_kernel(tiles, pos_ref, weight, scale, denom):
    tile, _ = place_of(tiles)
    denom[...] = jnp.zeros_like(denom)
    for parity, shifts in ((0, (-2, -1, 0, 1)), (1, (-1, 0, 1, 2))):
        for shift in shifts:
            inside, top_row, column = slot_of(pos_ref, tile, parity, tiles, shift)
            start = column - HALF - tile * TW

            @pl.when(inside & (start > -P_SIZE) & (start < TW))
            def _():
                base, extra = aligned(top_row)
                wide = lowered(weight[...], extra, 2 * P_SIZE)
                turned = pltpu.roll(wide, jnp.where(start < 0, start + 2 * P_SIZE, start), 1)
                denom[pl.ds(base, TALL), :] += turned[:, :TW]

    scale[...] = 1.0 / (denom[:OH] + 0.5)


ANY = pl.BlockSpec(memory_space=pl.ANY)
HBM = pl.BlockSpec(memory_space=pltpu.HBM)
VMEM = pl.BlockSpec(memory_space=pltpu.VMEM)
SMEM = pl.BlockSpec(memory_space=pltpu.SMEM)


def f32(*shape):
    return jax.ShapeDtypeStruct(shape, F32)


def limit(mib):
    return pltpu.CompilerParams(vmem_limit_bytes=mib * 2**20)


def cost(us):
    return pl.CostEstimate(flops=0, bytes_accessed=int(us * 3.5e6), transcendentals=0)


def local(intensity, positions, object_field, probe_modes, kernel_taps):
    tiles = lax.axis_size("tile")
    modes = lax.axis_size("mode")
    core = lax.rem(lax.axis_index("mode"), 2)
    spots = positions.T

    def along_x(array, steps):
        return lax.ppermute(array, "mode", [(i, (i + 2 * steps) % modes) for i in range(modes)])

    def swap(array):
        return lax.ppermute(array, "mode", [(i, i ^ 1) for i in range(modes)])

    def from_tile(array, step):
        pairs = []
        for tile in range(tiles):
            for mode in range(modes):
                source = tile + step if mode % 2 == 0 else tile - step
                if 0 <= source < tiles:
                    pairs.append((source * modes + mode, tile * modes + mode))
        return lax.ppermute(array, ("tile", "mode"), pairs)

    ring = [along_x(probe_modes, step) for step in (1, -1, 2)]
    halo, chosen = pl.pallas_call(
        pack_kernel,
        out_shape=(f32(2, OH, HALF), f32(P_SIZE, P_SIZE)),
        in_specs=[HBM, HBM],
        out_specs=(VMEM, VMEM),
        scratch_shapes=[pltpu.SemaphoreType.DMA((2,))],
        compiler_params=limit(4),
        cost_estimate=cost(2.2),
        name="pack",
    )(object_field, intensity)
    halo = from_tile(halo, 1)
    inward = from_tile(chosen, 1)
    outward = from_tile(chosen, -1)

    mine = pl.pallas_call(
        merge_kernel,
        out_shape=f32(MODES, P_SIZE, P_SIZE),
        in_specs=[ANY] * 4,
        out_specs=VMEM,
        scratch_shapes=[pltpu.SemaphoreType.DMA((4,))],
        compiler_params=limit(4),
        cost_estimate=cost(2.0),
        name="merge",
    )(probe_modes, *ring)
    mine, halo, inward, outward = lax.optimization_barrier((mine, halo, inward, outward))
    theirs = swap(mine)

    stages = [
        pltpu.VMEM((2 * P_SIZE, GROUP * P_SIZE), BF16),
        pltpu.VMEM((GROUP * P_SIZE, 2 * P_SIZE), BF16),
    ]
    far, patch, power, stacks = pl.pallas_call(
        functools.partial(first_kernel, tiles),
        out_shape=(
            f32(3, HELD, P_SIZE, 2 * P_SIZE),
            f32(3, 2, P_SIZE, P_SIZE),
            f32(3, P_SIZE, P_SIZE),
            jax.ShapeDtypeStruct((2, 2 * P_SIZE, 2 * P_SIZE), BF16),
        ),
        in_specs=[SMEM, VMEM, ANY, ANY, VMEM],
        out_specs=(VMEM,) * 4,
        scratch_shapes=[pltpu.VMEM((2, OH + 8, EXT), F32)]
        + stages
        + [pltpu.VMEM((8, 2 * P_SIZE), F32), pltpu.SemaphoreType.DMA((2,))],
        compiler_params=limit(20),
        cost_estimate=cost(6.0),
        name="far_of_own_modes",
    )(spots, kernel_taps, object_field, halo, mine)

    middle, rim, weight = pl.pallas_call(
        functools.partial(second_kernel, tiles),
        out_shape=(f32(2, OH, TW), f32(2, OH, HALF), f32(P_SIZE, P_SIZE)),
        in_specs=[SMEM] + [VMEM] * 9,
        out_specs=(VMEM,) * 3,
        scratch_shapes=[
            pltpu.VMEM((2, OH + 8, EXT), F32),
            pltpu.VMEM((3, P_SIZE, P_SIZE), F32),
            pltpu.VMEM((HELD, P_SIZE, 2 * P_SIZE), F32),
        ]
        + stages
        + [pltpu.VMEM((P_SIZE, P_SIZE), F32), pltpu.VMEM((2, P_SIZE, P_SIZE), F32)],
        compiler_params=limit(20),
        cost_estimate=cost(10.0),
        name="update_terms",
    )(spots, intensity, inward, outward, mine, theirs, far, patch, power, stacks)

    arrived = from_tile(rim, -1)
    scale = pl.pallas_call(
        functools.partial(denom_kernel, tiles),
        out_shape=f32(OH, TW),
        in_specs=[SMEM, VMEM],
        out_specs=VMEM,
        scratch_shapes=[pltpu.VMEM((OH + 8, TW), F32)],
        compiler_params=limit(4),
        cost_estimate=cost(3.5),
        name="denominator",
    )(spots, weight)
    blank = jnp.zeros_like(arrived)
    low = jnp.where(core == 0, arrived, blank)
    high = jnp.where(core == 0, blank, arrived)
    terms = (middle + jnp.concatenate([low, high], axis=2)) * scale
    return object_field + (terms + swap(terms))


def solution(mesh):
    return jax.shard_map(
        local,
        mesh=mesh,
        in_specs=(
            P("tile", None, None),
            P(),
            P(None, None, "tile"),
            P("mode", None, None, None),
            P(),
        ),
        out_specs=P(None, None, "tile"),
        check_vma=False,
    )
```

```python
import functools

import jax
import jax.numpy as jnp
from jax import lax
from jax.experimental import pallas as pl
from jax.experimental.pallas import tpu as pltpu
from jax.sharding import PartitionSpec as P

P_SIZE = 256
BAND = 64
TW = 256
HALF = 128
OH = 320
MODES = 8
EXT = TW + HALF
TALL = P_SIZE + 8
GROUP = 2
HELD = MODES // 2
F32 = jnp.float32
BF16 = jnp.bfloat16


def place_of(tiles):
    return lax.axis_index("tile"), lax.rem(lax.axis_index("mode"), 2)


def slot_of(pos_ref, tile, core, tiles, shift):
    block = tile + shift
    inside = (block >= 0) & (block < tiles)
    pattern = 2 * jnp.clip(block, 0, tiles - 1) + core
    return inside, pos_ref[0, pattern], pos_ref[1, pattern]


def aligned(top_row):
    extra = lax.rem(top_row, 8)
    return pl.multiple_of(top_row - extra, 8), extra


def lowered(window, extra, width):
    tall = jnp.concatenate([window, jnp.zeros((TALL - P_SIZE, P_SIZE), F32)], axis=0)
    return jnp.concatenate([pltpu.roll(tall, extra, 0), jnp.zeros((TALL, width - P_SIZE), F32)], axis=1)


def run_copies(moves, sem):
    copies = [pltpu.make_async_copy(src, dst, sem.at[i]) for i, (src, dst) in enumerate(moves)]
    for copy in copies:
        copy.start()
    for copy in copies:
        copy.wait()


def pack_kernel(obj, own, halo, merged, sem):
    core = lax.rem(lax.axis_index("mode"), 2)
    edge = pl.ds(pl.multiple_of(core * HALF, HALF), HALF)
    run_copies([(obj.at[:, :, edge], halo), (own.at[0], merged.at[0:2])], sem)


def merge_kernel(before, first, second, third, inward, merged, sem):
    del before
    core = lax.rem(lax.axis_index("mode"), 2)
    moves = [(array.at[0], merged.at[2 * i + 2 : 2 * i + 4]) for i, array in enumerate((first, second, third))]
    moves.append((inward.at[1 - core], merged.at[MODES]))
    run_copies(moves, sem)


def window_of(pos_ref, tiles, slot):
    tile, core = place_of(tiles)
    inside, top_row, column = slot_of(pos_ref, tile, core, tiles, (slot - 1) * (1 - 2 * core))
    offset = column - tile * TW - (1 - core) * HALF
    here = inside & (column >= tile * TW) & (column < (tile + 1) * TW)
    return here, top_row, offset


def columns_of(unit):
    return slice(unit * P_SIZE, (unit + 1) * P_SIZE)


def mix(first, second, low, midb, units):
    width = units * P_SIZE
    mid = jnp.dot(first, low[:, :width], preferred_element_type=F32)
    for unit in range(units):
        own = columns_of(unit)
        midb[own, :P_SIZE] = mid[:P_SIZE, own].astype(BF16)
        midb[own, P_SIZE:] = mid[P_SIZE:, own].astype(BF16)
    return jnp.dot(midb[:width], second, preferred_element_type=F32)


def forward(probe, modes, patch_re, patch_im, stacks, low, midb, far, power):
    for unit, mode in enumerate(modes):
        own = columns_of(unit)
        pr = probe[2 * mode]
        pi = probe[2 * mode + 1]
        low[:P_SIZE, own] = (pr * patch_re[...] - pi * patch_im[...]).astype(BF16)
        low[P_SIZE:, own] = (pr * patch_im[...] + pi * patch_re[...]).astype(BF16)
    out = mix(stacks[0], stacks[1], low, midb, len(modes))
    for unit in range(len(modes)):
        block = out[columns_of(unit)]
        far[unit] = block
        power[...] += block[:, :P_SIZE] * block[:, :P_SIZE] + block[:, P_SIZE:] * block[:, P_SIZE:]


def window_kernel(tiles, pos_ref, taps_ref, obj, halo, own, patch, stacks, far, power, wave, low, midb, row_pad, sem):
    _, core = place_of(tiles)
    rim = pl.ds(pl.multiple_of((1 - core) * TW, HALF), HALF)
    moves = (
        (obj, wave.at[:, :OH, pl.ds(pl.multiple_of(core * HALF, HALF), TW)]),
        (halo, wave.at[:, :OH, rim]),
    )
    copies = [pltpu.make_async_copy(src, dst, sem.at[i]) for i, (src, dst) in enumerate(moves)]
    for copy in copies:
        copy.start()

    row_pad[...] = jnp.zeros_like(row_pad)
    row_pad[0:2, 0 : 2 * BAND + 1] = taps_ref[...]

    def band(part):
        line = jnp.broadcast_to(row_pad[part : part + 1, :], (P_SIZE, 2 * P_SIZE))
        turned = pltpu.roll(line, 2 * P_SIZE - BAND, 1, stride=1, stride_axis=0)
        return turned[:, :P_SIZE]

    band_re = band(0)
    band_im = band(1)
    turned_re = band_re.T
    turned_im = band_im.T
    for which, blocks in enumerate(((band_re, -band_im, band_im), (turned_re, turned_im, -turned_im))):
        stacks[which, :P_SIZE, :P_SIZE] = blocks[0].astype(BF16)
        stacks[which, :P_SIZE, P_SIZE:] = blocks[1].astype(BF16)
        stacks[which, P_SIZE:, :P_SIZE] = blocks[2].astype(BF16)
        stacks[which, P_SIZE:, P_SIZE:] = blocks[0].astype(BF16)

    for copy in copies:
        copy.wait()

    @pl.loop(0, 3)
    def _(slot):
        here, top_row, offset = window_of(pos_ref, tiles, slot)

        @pl.when(here)
        def _():
            base, extra = aligned(top_row)
            for part in range(2):
                rows = wave[part, pl.ds(base, TALL), :]
                turned = pltpu.roll(rows, lax.rem(EXT - offset, EXT), 1)[:, :P_SIZE]
                patch[slot, part] = pltpu.roll(turned, lax.rem(TALL - extra, TALL), 0)[:P_SIZE]
            power[slot] = jnp.zeros((P_SIZE, P_SIZE), F32)
            forward(own.at[0], (0,), patch.at[slot, 0], patch.at[slot, 1], stacks, low, midb, far.at[slot], power.at[slot])


def first_kernel(tiles, pos_ref, mine, patch, stacks, before, far, power, low, midb):
    @pl.loop(0, 3)
    def _(slot):
        here, _, _ = window_of(pos_ref, tiles, slot)

        @pl.when(here)
        def _():
            power[slot] = before[slot]
            sides = (patch.at[slot, 0], patch.at[slot, 1])
            forward(mine, (1, 2, 3), *sides, stacks, low, midb, far.at[slot], power.at[slot])


def second_kernel(
    tiles, pos_ref, inten, inward, mine, theirs, far_own, far_ring, patch, power, stacks, mid_out, rim_out, weight,
    total, meas, far_too, low, midb, ratio, acc,
):
    _, core = place_of(tiles)
    total[...] = jnp.zeros_like(total)
    meas[0] = theirs[MODES]
    meas[1] = inten[core]
    meas[2] = inward[core]
    weight[...] = jnp.zeros_like(weight)

    @pl.loop(0, MODES)
    def _(plane):
        weight[...] += mine[plane] * mine[plane] + theirs[plane] * theirs[plane]

    @pl.loop(0, 3)
    def _(slot):
        here, top_row, offset = window_of(pos_ref, tiles, slot)

        @pl.when(here)
        def _():
            base, extra = aligned(top_row)
            ratio[...] = power[slot]
            sides = (patch.at[slot, 0], patch.at[slot, 1])
            forward(theirs, (0, 1), *sides, stacks, low, midb, far_too.at[0:2], ratio)
            forward(theirs, (2, 3), *sides, stacks, low, midb, far_too.at[2:4], ratio)
            ratio[...] = jnp.sqrt(meas[slot]) / jnp.sqrt(ratio[...] + 1.0)
            acc[0] = -weight[...] * patch[slot, 0]
            acc[1] = -weight[...] * patch[slot, 1]
            fields = [(far_own.at[slot, 0], mine, 0)]
            fields += [(far_ring.at[slot, i], mine, i + 1) for i in range(3)]
            fields += [(far_too.at[i], theirs, i) for i in range(HELD)]
            for start in range(0, MODES, GROUP):
                group = fields[start : start + GROUP]
                for unit, (source, _, _) in enumerate(group):
                    own = columns_of(unit)
                    low[:P_SIZE, own] = (source[:, :P_SIZE] * ratio[...]).astype(BF16)
                    low[P_SIZE:, own] = (source[:, P_SIZE:] * ratio[...]).astype(BF16)
                out = mix(stacks[1], stacks[0], low, midb, GROUP)
                term_re = 0.0
                term_im = 0.0
                for unit, (_, probe, mode) in enumerate(group):
                    back_re = out[columns_of(unit), :P_SIZE]
                    back_im = out[columns_of(unit), P_SIZE:]
                    pr = probe[2 * mode]
                    pi = probe[2 * mode + 1]
                    term_re += pr * back_re + pi * back_im
                    term_im += pr * back_im - pi * back_re
                acc[0] += term_re
                acc[1] += term_im

            for part in range(2):
                total[part, pl.ds(base, TALL), :] += pltpu.roll(lowered(acc[part], extra, EXT), offset, 1)

    mid_out[...] = total[:, :OH, pl.ds(pl.multiple_of(core * HALF, HALF), TW)]
    rim_out[...] = total[:, :OH, pl.ds(pl.multiple_of((1 - core) * TW, HALF), HALF)]


def denom_kernel(tiles, pos_ref, weight, scale, denom):
    tile, _ = place_of(tiles)
    denom[...] = jnp.zeros_like(denom)
    for parity, shifts in ((0, (-2, -1, 0, 1)), (1, (-1, 0, 1, 2))):
        for shift in shifts:
            inside, top_row, column = slot_of(pos_ref, tile, parity, tiles, shift)
            start = column - HALF - tile * TW

            @pl.when(inside & (start > -P_SIZE) & (start < TW))
            def _():
                base, extra = aligned(top_row)
                wide = lowered(weight[...], extra, 2 * P_SIZE)
                turned = pltpu.roll(wide, jnp.where(start < 0, start + 2 * P_SIZE, start), 1)
                denom[pl.ds(base, TALL), :] += turned[:, :TW]

    scale[...] = 1.0 / (denom[:OH] + 0.5)


ANY = pl.BlockSpec(memory_space=pl.ANY)
HBM = pl.BlockSpec(memory_space=pltpu.HBM)
VMEM = pl.BlockSpec(memory_space=pltpu.VMEM)
SMEM = pl.BlockSpec(memory_space=pltpu.SMEM)


def f32(*shape):
    return jax.ShapeDtypeStruct(shape, F32)


def limit(mib):
    return pltpu.CompilerParams(vmem_limit_bytes=mib * 2**20)


def cost(us):
    return pl.CostEstimate(flops=0, bytes_accessed=int(us * 3.5e6), transcendentals=0)


def local(intensity, positions, object_field, probe_modes, kernel_taps):
    tiles = lax.axis_size("tile")
    modes = lax.axis_size("mode")
    core = lax.rem(lax.axis_index("mode"), 2)
    spots = positions.T

    def along_x(array, steps):
        return lax.ppermute(array, "mode", [(i, (i + 2 * steps) % modes) for i in range(modes)])

    def swap(array):
        return lax.ppermute(array, "mode", [(i, i ^ 1) for i in range(modes)])

    def from_tile(array, step):
        pairs = []
        for tile in range(tiles):
            for mode in range(modes):
                source = tile + step if mode % 2 == 0 else tile - step
                if 0 <= source < tiles:
                    pairs.append((source * modes + mode, tile * modes + mode))
        return lax.ppermute(array, ("tile", "mode"), pairs)

    ring = [along_x(probe_modes, step) for step in (1, -1, 2)]
    halo, held = pl.pallas_call(
        pack_kernel,
        out_shape=(f32(2, OH, HALF), f32(MODES + 1, P_SIZE, P_SIZE)),
        in_specs=[ANY, ANY],
        out_specs=(VMEM, VMEM),
        scratch_shapes=[pltpu.SemaphoreType.DMA((2,))],
        compiler_params=limit(4),
        cost_estimate=cost(2.2),
        name="pack",
    )(object_field, probe_modes)
    halo = from_tile(halo, 1)
    inward = from_tile(intensity, 1)

    def stages(units):
        return [
            pltpu.VMEM((2 * P_SIZE, units * P_SIZE), BF16),
            pltpu.VMEM((units * P_SIZE, 2 * P_SIZE), BF16),
        ]

    patch, stacks, far_own, power = pl.pallas_call(
        functools.partial(window_kernel, tiles),
        out_shape=(
            f32(3, 2, P_SIZE, P_SIZE),
            jax.ShapeDtypeStruct((2, 2 * P_SIZE, 2 * P_SIZE), BF16),
            f32(3, 1, P_SIZE, 2 * P_SIZE),
            f32(3, P_SIZE, P_SIZE),
        ),
        in_specs=[SMEM, VMEM, ANY, ANY, VMEM],
        out_specs=(VMEM,) * 4,
        scratch_shapes=[pltpu.VMEM((2, OH + 8, EXT), F32)]
        + stages(1)
        + [pltpu.VMEM((8, 2 * P_SIZE), F32), pltpu.SemaphoreType.DMA((2,))],
        compiler_params=limit(16),
        cost_estimate=cost(4.0),
        name="windows",
    )(spots, kernel_taps, object_field, halo, probe_modes)

    mine = pl.pallas_call(
        merge_kernel,
        out_shape=f32(MODES + 1, P_SIZE, P_SIZE),
        in_specs=[ANY] * 5,
        out_specs=ANY,
        scratch_shapes=[pltpu.SemaphoreType.DMA((4,))],
        input_output_aliases={0: 0},
        compiler_params=limit(4),
        cost_estimate=cost(1.0),
        name="merge",
    )(held, *ring, inward)
    mine, patch, stacks, far_own, power = lax.optimization_barrier((mine, patch, stacks, far_own, power))
    theirs = swap(mine)

    far_ring, power = pl.pallas_call(
        functools.partial(first_kernel, tiles),
        out_shape=(f32(3, 3, P_SIZE, 2 * P_SIZE), f32(3, P_SIZE, P_SIZE)),
        in_specs=[SMEM] + [VMEM] * 4,
        out_specs=(VMEM,) * 2,
        scratch_shapes=stages(3),
        compiler_params=limit(16),
        cost_estimate=cost(4.0),
        name="far_of_own_modes",
    )(spots, mine, patch, stacks, power)

    middle, rim, weight = pl.pallas_call(
        functools.partial(second_kernel, tiles),
        out_shape=(f32(2, OH, TW), f32(2, OH, HALF), f32(P_SIZE, P_SIZE)),
        in_specs=[SMEM] + [VMEM] * 9,
        out_specs=(VMEM,) * 3,
        scratch_shapes=[
            pltpu.VMEM((2, OH + 8, EXT), F32),
            pltpu.VMEM((3, P_SIZE, P_SIZE), F32),
            pltpu.VMEM((HELD, P_SIZE, 2 * P_SIZE), F32),
        ]
        + stages(GROUP)
        + [pltpu.VMEM((P_SIZE, P_SIZE), F32), pltpu.VMEM((2, P_SIZE, P_SIZE), F32)],
        compiler_params=limit(20),
        cost_estimate=cost(10.0),
        name="update_terms",
    )(spots, intensity, inward, mine, theirs, far_own, far_ring, patch, power, stacks)

    arrived = from_tile(rim, -1)
    scale = pl.pallas_call(
        functools.partial(denom_kernel, tiles),
        out_shape=f32(OH, TW),
        in_specs=[SMEM, VMEM],
        out_specs=VMEM,
        scratch_shapes=[pltpu.VMEM((OH + 8, TW), F32)],
        compiler_params=limit(4),
        cost_estimate=cost(3.5),
        name="denominator",
    )(spots, weight)
    blank = jnp.zeros_like(arrived)
    low = jnp.where(core == 0, arrived, blank)
    high = jnp.where(core == 0, blank, arrived)
    terms = (middle + jnp.concatenate([low, high], axis=2)) * scale
    return object_field + (terms + swap(terms))


def solution(mesh):
    return jax.shard_map(
        local,
        mesh=mesh,
        in_specs=(
            P("tile", None, None),
            P(),
            P(None, None, "tile"),
            P("mode", None, None, None),
            P(),
        ),
        out_specs=P(None, None, "tile"),
        check_vma=False,
    )
```

```python
import functools

import jax
import jax.numpy as jnp
from jax import lax
from jax.experimental import pallas as pl
from jax.experimental.pallas import tpu as pltpu
from jax.sharding import PartitionSpec as P

P_SIZE = 256
BAND = 64
TW = 256
HALF = 128
OH = 320
MODES = 8
EXT = TW + HALF
TALL = P_SIZE + 8
GROUP = 2
HELD = MODES // 2
F32 = jnp.float32
BF16 = jnp.bfloat16


def place_of(tiles):
    return lax.axis_index("tile"), lax.rem(lax.axis_index("mode"), 2)


def slot_of(pos_ref, tile, core, tiles, shift):
    block = tile + shift
    inside = (block >= 0) & (block < tiles)
    pattern = 2 * jnp.clip(block, 0, tiles - 1) + core
    return inside, pos_ref[0, pattern], pos_ref[1, pattern]


def aligned(top_row):
    extra = lax.rem(top_row, 8)
    return pl.multiple_of(top_row - extra, 8), extra


def lowered(window, extra, width):
    tall = jnp.concatenate([window, jnp.zeros((TALL - P_SIZE, P_SIZE), F32)], axis=0)
    return jnp.concatenate([pltpu.roll(tall, extra, 0), jnp.zeros((TALL, width - P_SIZE), F32)], axis=1)


def run_copies(moves, sem):
    copies = [pltpu.make_async_copy(src, dst, sem.at[i]) for i, (src, dst) in enumerate(moves)]
    for copy in copies:
        copy.start()
    for copy in copies:
        copy.wait()


def merge_kernel(own, first, second, third, inward, merged, sem):
    core = lax.rem(lax.axis_index("mode"), 2)
    moves = [(array.at[0], merged.at[2 * i : 2 * i + 2]) for i, array in enumerate((own, first, second, third))]
    moves.append((inward.at[1 - core], merged.at[MODES]))
    run_copies(moves, sem)


def window_of(pos_ref, tiles, slot):
    tile, core = place_of(tiles)
    inside, top_row, column = slot_of(pos_ref, tile, core, tiles, (slot - 1) * (1 - 2 * core))
    offset = column - tile * TW - (1 - core) * HALF
    here = inside & (column >= tile * TW) & (column < (tile + 1) * TW)
    return here, top_row, offset


def columns_of(unit):
    return slice(unit * P_SIZE, (unit + 1) * P_SIZE)


def mix(first, second, low, midb, units):
    width = units * P_SIZE
    mid = jnp.dot(first, low[:, :width], preferred_element_type=F32)
    for unit in range(units):
        own = columns_of(unit)
        midb[own, :P_SIZE] = mid[:P_SIZE, own].astype(BF16)
        midb[own, P_SIZE:] = mid[P_SIZE:, own].astype(BF16)
    return jnp.dot(midb[:width], second, preferred_element_type=F32)


def forward(probe, modes, patch_re, patch_im, stacks, low, midb, far, power):
    for unit, mode in enumerate(modes):
        own = columns_of(unit)
        pr = probe[2 * mode]
        pi = probe[2 * mode + 1]
        low[:P_SIZE, own] = (pr * patch_re[...] - pi * patch_im[...]).astype(BF16)
        low[P_SIZE:, own] = (pr * patch_im[...] + pi * patch_re[...]).astype(BF16)
    out = mix(stacks[0], stacks[1], low, midb, len(modes))
    for unit in range(len(modes)):
        block = out[columns_of(unit)]
        far[unit] = block
        power[...] += block[:, :P_SIZE] * block[:, :P_SIZE] + block[:, P_SIZE:] * block[:, P_SIZE:]


def window_kernel(tiles, pos_ref, taps_ref, obj, beside, own, patch, stacks, far, power, wave, low, midb, row_pad, sem):
    _, core = place_of(tiles)
    rim = pl.ds(pl.multiple_of((1 - core) * TW, HALF), HALF)
    moves = (
        (obj, wave.at[:, :OH, pl.ds(pl.multiple_of(core * HALF, HALF), TW)]),
        (beside.at[:, :, pl.ds(pl.multiple_of(core * HALF, HALF), HALF)], wave.at[:, :OH, rim]),
    )
    copies = [pltpu.make_async_copy(src, dst, sem.at[i]) for i, (src, dst) in enumerate(moves)]
    for copy in copies:
        copy.start()

    row_pad[...] = jnp.zeros_like(row_pad)
    row_pad[0:2, 0 : 2 * BAND + 1] = taps_ref[...]

    def band(part):
        line = jnp.broadcast_to(row_pad[part : part + 1, :], (P_SIZE, 2 * P_SIZE))
        turned = pltpu.roll(line, 2 * P_SIZE - BAND, 1, stride=1, stride_axis=0)
        return turned[:, :P_SIZE]

    band_re = band(0)
    band_im = band(1)
    turned_re = band_re.T
    turned_im = band_im.T
    for which, blocks in enumerate(((band_re, -band_im, band_im), (turned_re, turned_im, -turned_im))):
        stacks[which, :P_SIZE, :P_SIZE] = blocks[0].astype(BF16)
        stacks[which, :P_SIZE, P_SIZE:] = blocks[1].astype(BF16)
        stacks[which, P_SIZE:, :P_SIZE] = blocks[2].astype(BF16)
        stacks[which, P_SIZE:, P_SIZE:] = blocks[0].astype(BF16)

    for copy in copies:
        copy.wait()

    @pl.loop(0, 3)
    def _(slot):
        here, top_row, offset = window_of(pos_ref, tiles, slot)

        @pl.when(here)
        def _():
            base, extra = aligned(top_row)
            for part in range(2):
                rows = wave[part, pl.ds(base, TALL), :]
                turned = pltpu.roll(rows, lax.rem(EXT - offset, EXT), 1)[:, :P_SIZE]
                patch[slot, part] = pltpu.roll(turned, lax.rem(TALL - extra, TALL), 0)[:P_SIZE]
            power[slot] = jnp.zeros((P_SIZE, P_SIZE), F32)
            forward(own.at[0], (0,), patch.at[slot, 0], patch.at[slot, 1], stacks, low, midb, far.at[slot], power.at[slot])


def first_kernel(tiles, pos_ref, mine, patch, stacks, before, far, power, low, midb):
    @pl.loop(0, 3)
    def _(slot):
        here, _, _ = window_of(pos_ref, tiles, slot)

        @pl.when(here)
        def _():
            power[slot] = before[slot]
            sides = (patch.at[slot, 0], patch.at[slot, 1])
            forward(mine, (1, 2, 3), *sides, stacks, low, midb, far.at[slot], power.at[slot])


def second_kernel(
    tiles, pos_ref, inten, inward, mine, theirs, far_own, far_ring, patch, power, stacks, mid_out, rim_out, weight,
    total, meas, far_too, low, midb, ratio, acc,
):
    _, core = place_of(tiles)
    total[...] = jnp.zeros_like(total)
    meas[0] = theirs[MODES]
    meas[1] = inten[core]
    meas[2] = inward[core]
    weight[...] = jnp.zeros_like(weight)

    @pl.loop(0, MODES)
    def _(plane):
        weight[...] += mine[plane] * mine[plane] + theirs[plane] * theirs[plane]

    @pl.loop(0, 3)
    def _(slot):
        here, top_row, offset = window_of(pos_ref, tiles, slot)

        @pl.when(here)
        def _():
            base, extra = aligned(top_row)
            ratio[...] = power[slot]
            sides = (patch.at[slot, 0], patch.at[slot, 1])
            forward(theirs, (0, 1), *sides, stacks, low, midb, far_too.at[0:2], ratio)
            forward(theirs, (2, 3), *sides, stacks, low, midb, far_too.at[2:4], ratio)
            ratio[...] = jnp.sqrt(meas[slot]) / jnp.sqrt(ratio[...] + 1.0)
            acc[0] = -weight[...] * patch[slot, 0]
            acc[1] = -weight[...] * patch[slot, 1]
            fields = [(far_own.at[slot, 0], mine, 0)]
            fields += [(far_ring.at[slot, i], mine, i + 1) for i in range(3)]
            fields += [(far_too.at[i], theirs, i) for i in range(HELD)]
            for start in range(0, MODES, GROUP):
                group = fields[start : start + GROUP]
                for unit, (source, _, _) in enumerate(group):
                    own = columns_of(unit)
                    low[:P_SIZE, own] = (source[:, :P_SIZE] * ratio[...]).astype(BF16)
                    low[P_SIZE:, own] = (source[:, P_SIZE:] * ratio[...]).astype(BF16)
                out = mix(stacks[1], stacks[0], low, midb, GROUP)
                term_re = 0.0
                term_im = 0.0
                for unit, (_, probe, mode) in enumerate(group):
                    back_re = out[columns_of(unit), :P_SIZE]
                    back_im = out[columns_of(unit), P_SIZE:]
                    pr = probe[2 * mode]
                    pi = probe[2 * mode + 1]
                    term_re += pr * back_re + pi * back_im
                    term_im += pr * back_im - pi * back_re
                acc[0] += term_re
                acc[1] += term_im

            for part in range(2):
                total[part, pl.ds(base, TALL), :] += pltpu.roll(lowered(acc[part], extra, EXT), offset, 1)

    mid_out[...] = total[:, :OH, pl.ds(pl.multiple_of(core * HALF, HALF), TW)]
    rim_out[...] = total[:, :OH, pl.ds(pl.multiple_of((1 - core) * TW, HALF), HALF)]


def denom_kernel(tiles, pos_ref, weight, scale, denom):
    tile, _ = place_of(tiles)
    denom[...] = jnp.zeros_like(denom)
    for parity, shifts in ((0, (-2, -1, 0, 1)), (1, (-1, 0, 1, 2))):
        for shift in shifts:
            inside, top_row, column = slot_of(pos_ref, tile, parity, tiles, shift)
            start = column - HALF - tile * TW

            @pl.when(inside & (start > -P_SIZE) & (start < TW))
            def _():
                base, extra = aligned(top_row)
                wide = lowered(weight[...], extra, 2 * P_SIZE)
                turned = pltpu.roll(wide, jnp.where(start < 0, start + 2 * P_SIZE, start), 1)
                denom[pl.ds(base, TALL), :] += turned[:, :TW]

    scale[...] = 1.0 / (denom[:OH] + 0.5)


ANY = pl.BlockSpec(memory_space=pl.ANY)
HBM = pl.BlockSpec(memory_space=pltpu.HBM)
VMEM = pl.BlockSpec(memory_space=pltpu.VMEM)
SMEM = pl.BlockSpec(memory_space=pltpu.SMEM)


def f32(*shape):
    return jax.ShapeDtypeStruct(shape, F32)


def limit(mib):
    return pltpu.CompilerParams(vmem_limit_bytes=mib * 2**20)


def cost(us):
    return pl.CostEstimate(flops=0, bytes_accessed=int(us * 3.5e6), transcendentals=0)


def local(intensity, positions, object_field, probe_modes, kernel_taps):
    tiles = lax.axis_size("tile")
    modes = lax.axis_size("mode")
    core = lax.rem(lax.axis_index("mode"), 2)
    spots = positions.T

    def along_x(array, steps):
        return lax.ppermute(array, "mode", [(i, (i + 2 * steps) % modes) for i in range(modes)])

    def swap(array):
        return lax.ppermute(array, "mode", [(i, i ^ 1) for i in range(modes)])

    def from_tile(array, step):
        pairs = []
        for tile in range(tiles):
            for mode in range(modes):
                source = tile + step if mode % 2 == 0 else tile - step
                if 0 <= source < tiles:
                    pairs.append((source * modes + mode, tile * modes + mode))
        return lax.ppermute(array, ("tile", "mode"), pairs)

    ring = [along_x(probe_modes, step) for step in (1, -1, 2)]
    beside = from_tile(object_field, 1)
    inward = from_tile(intensity, 1)

    def stages(units):
        return [
            pltpu.VMEM((2 * P_SIZE, units * P_SIZE), BF16),
            pltpu.VMEM((units * P_SIZE, 2 * P_SIZE), BF16),
        ]

    patch, stacks, far_own, power = pl.pallas_call(
        functools.partial(window_kernel, tiles),
        out_shape=(
            f32(3, 2, P_SIZE, P_SIZE),
            jax.ShapeDtypeStruct((2, 2 * P_SIZE, 2 * P_SIZE), BF16),
            f32(3, 1, P_SIZE, 2 * P_SIZE),
            f32(3, P_SIZE, P_SIZE),
        ),
        in_specs=[SMEM, VMEM, ANY, ANY, VMEM],
        out_specs=(VMEM,) * 4,
        scratch_shapes=[pltpu.VMEM((2, OH + 8, EXT), F32)]
        + stages(1)
        + [pltpu.VMEM((8, 2 * P_SIZE), F32), pltpu.SemaphoreType.DMA((2,))],
        compiler_params=limit(16),
        cost_estimate=cost(4.0),
        name="windows",
    )(spots, kernel_taps, object_field, beside, probe_modes)

    held, inward, patch, stacks, far_own, power = lax.optimization_barrier(
        (probe_modes, inward, patch, stacks, far_own, power)
    )
    mine = pl.pallas_call(
        merge_kernel,
        out_shape=f32(MODES + 1, P_SIZE, P_SIZE),
        in_specs=[ANY] * 5,
        out_specs=VMEM,
        scratch_shapes=[pltpu.SemaphoreType.DMA((5,))],
        compiler_params=limit(4),
        cost_estimate=cost(1.0),
        name="merge",
    )(held, *ring, inward)
    theirs = swap(mine)

    far_ring, power = pl.pallas_call(
        functools.partial(first_kernel, tiles),
        out_shape=(f32(3, 3, P_SIZE, 2 * P_SIZE), f32(3, P_SIZE, P_SIZE)),
        in_specs=[SMEM] + [VMEM] * 4,
        out_specs=(VMEM,) * 2,
        scratch_shapes=stages(3),
        compiler_params=limit(16),
        cost_estimate=cost(4.0),
        name="far_of_own_modes",
    )(spots, mine, patch, stacks, power)

    middle, rim, weight = pl.pallas_call(
        functools.partial(second_kernel, tiles),
        out_shape=(f32(2, OH, TW), f32(2, OH, HALF), f32(P_SIZE, P_SIZE)),
        in_specs=[SMEM] + [VMEM] * 9,
        out_specs=(VMEM,) * 3,
        scratch_shapes=[
            pltpu.VMEM((2, OH + 8, EXT), F32),
            pltpu.VMEM((3, P_SIZE, P_SIZE), F32),
            pltpu.VMEM((HELD, P_SIZE, 2 * P_SIZE), F32),
        ]
        + stages(GROUP)
        + [pltpu.VMEM((P_SIZE, P_SIZE), F32), pltpu.VMEM((2, P_SIZE, P_SIZE), F32)],
        compiler_params=limit(20),
        cost_estimate=cost(10.0),
        name="update_terms",
    )(spots, intensity, inward, mine, theirs, far_own, far_ring, patch, power, stacks)

    arrived = from_tile(rim, -1)
    scale = pl.pallas_call(
        functools.partial(denom_kernel, tiles),
        out_shape=f32(OH, TW),
        in_specs=[SMEM, VMEM],
        out_specs=VMEM,
        scratch_shapes=[pltpu.VMEM((OH + 8, TW), F32)],
        compiler_params=limit(4),
        cost_estimate=cost(3.5),
        name="denominator",
    )(spots, weight)
    blank = jnp.zeros_like(arrived)
    low = jnp.where(core == 0, arrived, blank)
    high = jnp.where(core == 0, blank, arrived)
    terms = (middle + jnp.concatenate([low, high], axis=2)) * scale
    return object_field + (terms + swap(terms))


def solution(mesh):
    return jax.shard_map(
        local,
        mesh=mesh,
        in_specs=(
            P("tile", None, None),
            P(),
            P(None, None, "tile"),
            P("mode", None, None, None),
            P(),
        ),
        out_specs=P(None, None, "tile"),
        check_vma=False,
    )
```

```python
import functools

import jax
import jax.numpy as jnp
from jax import lax
from jax.experimental import pallas as pl
from jax.experimental.pallas import tpu as pltpu
from jax.sharding import PartitionSpec as P

P_SIZE = 256
BAND = 64
TW = 256
HALF = 128
OH = 320
MODES = 8
EXT = TW + HALF
TALL = P_SIZE + 8
GROUP = 2
HELD = MODES // 2
F32 = jnp.float32
BF16 = jnp.bfloat16


def place_of(tiles):
    return lax.axis_index("tile"), lax.rem(lax.axis_index("mode"), 2)


def slot_of(pos_ref, tile, core, tiles, shift):
    block = tile + shift
    inside = (block >= 0) & (block < tiles)
    pattern = 2 * jnp.clip(block, 0, tiles - 1) + core
    return inside, pos_ref[0, pattern], pos_ref[1, pattern]


def aligned(top_row):
    extra = lax.rem(top_row, 8)
    return pl.multiple_of(top_row - extra, 8), extra


def lowered(window, extra, width):
    tall = jnp.concatenate([window, jnp.zeros((TALL - P_SIZE, P_SIZE), F32)], axis=0)
    return jnp.concatenate([pltpu.roll(tall, extra, 0), jnp.zeros((TALL, width - P_SIZE), F32)], axis=1)


def run_copies(moves, sem):
    copies = [pltpu.make_async_copy(src, dst, sem.at[i]) for i, (src, dst) in enumerate(moves)]
    for copy in copies:
        copy.start()
    for copy in copies:
        copy.wait()


def pack_kernel(obj, own, halo, merged, sem):
    core = lax.rem(lax.axis_index("mode"), 2)
    edge = pl.ds(pl.multiple_of(core * HALF, HALF), HALF)
    run_copies([(obj.at[:, :, edge], halo), (own.at[0], merged.at[0:2])], sem)


def merge_kernel(before, first, second, third, merged, sem):
    del before
    arrays = (first, second, third)
    run_copies([(array.at[0], merged.at[2 * i + 2 : 2 * i + 4]) for i, array in enumerate(arrays)], sem)


def append_kernel(inward, before, merged, sem):
    del before
    core = lax.rem(lax.axis_index("mode"), 2)
    run_copies([(inward.at[1 - core], merged.at[MODES])], sem)


def window_of(pos_ref, tiles, slot):
    tile, core = place_of(tiles)
    inside, top_row, column = slot_of(pos_ref, tile, core, tiles, (slot - 1) * (1 - 2 * core))
    offset = column - tile * TW - (1 - core) * HALF
    here = inside & (column >= tile * TW) & (column < (tile + 1) * TW)
    return here, top_row, offset


def columns_of(unit):
    return slice(unit * P_SIZE, (unit + 1) * P_SIZE)


def mix(first, second, low, midb, units):
    width = units * P_SIZE
    mid = jnp.dot(first, low[:, :width], preferred_element_type=F32)
    for unit in range(units):
        own = columns_of(unit)
        midb[own, :P_SIZE] = mid[:P_SIZE, own].astype(BF16)
        midb[own, P_SIZE:] = mid[P_SIZE:, own].astype(BF16)
    return jnp.dot(midb[:width], second, preferred_element_type=F32)


def forward(probe, modes, patch_re, patch_im, stacks, low, midb, far, power):
    for unit, mode in enumerate(modes):
        own = columns_of(unit)
        pr = probe[2 * mode]
        pi = probe[2 * mode + 1]
        low[:P_SIZE, own] = (pr * patch_re[...] - pi * patch_im[...]).astype(BF16)
        low[P_SIZE:, own] = (pr * patch_im[...] + pi * patch_re[...]).astype(BF16)
    out = mix(stacks[0], stacks[1], low, midb, len(modes))
    for unit in range(len(modes)):
        block = out[columns_of(unit)]
        far[unit] = block
        power[...] += block[:, :P_SIZE] * block[:, :P_SIZE] + block[:, P_SIZE:] * block[:, P_SIZE:]


def first_kernel(tiles, pos_ref, taps_ref, obj, beside, mine, patch, stacks, far, power, wave, low, midb, row_pad, sem):
    _, core = place_of(tiles)
    rim = pl.ds(pl.multiple_of((1 - core) * TW, HALF), HALF)
    moves = (
        (obj, wave.at[:, :OH, pl.ds(pl.multiple_of(core * HALF, HALF), TW)]),
        (beside, wave.at[:, :OH, rim]),
    )
    copies = [pltpu.make_async_copy(src, dst, sem.at[i]) for i, (src, dst) in enumerate(moves)]
    for copy in copies:
        copy.start()

    row_pad[...] = jnp.zeros_like(row_pad)
    row_pad[0:2, 0 : 2 * BAND + 1] = taps_ref[...]

    def band(part):
        line = jnp.broadcast_to(row_pad[part : part + 1, :], (P_SIZE, 2 * P_SIZE))
        turned = pltpu.roll(line, 2 * P_SIZE - BAND, 1, stride=1, stride_axis=0)
        return turned[:, :P_SIZE]

    band_re = band(0)
    band_im = band(1)
    turned_re = band_re.T
    turned_im = band_im.T
    for which, blocks in enumerate(((band_re, -band_im, band_im), (turned_re, turned_im, -turned_im))):
        stacks[which, :P_SIZE, :P_SIZE] = blocks[0].astype(BF16)
        stacks[which, :P_SIZE, P_SIZE:] = blocks[1].astype(BF16)
        stacks[which, P_SIZE:, :P_SIZE] = blocks[2].astype(BF16)
        stacks[which, P_SIZE:, P_SIZE:] = blocks[0].astype(BF16)

    for copy in copies:
        copy.wait()

    @pl.loop(0, 3)
    def _(slot):
        here, top_row, offset = window_of(pos_ref, tiles, slot)

        @pl.when(here)
        def _():
            base, extra = aligned(top_row)
            for part in range(2):
                rows = wave[part, pl.ds(base, TALL), :]
                turned = pltpu.roll(rows, lax.rem(EXT - offset, EXT), 1)[:, :P_SIZE]
                patch[slot, part] = pltpu.roll(turned, lax.rem(TALL - extra, TALL), 0)[:P_SIZE]
            power[slot] = jnp.zeros((P_SIZE, P_SIZE), F32)
            sides = (patch.at[slot, 0], patch.at[slot, 1])
            forward(mine, (0, 1), *sides, stacks, low, midb, far.at[slot, 0:2], power.at[slot])
            forward(mine, (2, 3), *sides, stacks, low, midb, far.at[slot, 2:4], power.at[slot])


def second_kernel(
    tiles, pos_ref, inten, inward, mine, theirs, far, patch, power, stacks, mid_out, rim_out, weight,
    total, meas, far_too, low, midb, ratio, acc,
):
    _, core = place_of(tiles)
    total[...] = jnp.zeros_like(total)
    meas[0] = theirs[MODES]
    meas[1] = inten[core]
    meas[2] = inward[core]
    weight[...] = jnp.zeros_like(weight)

    @pl.loop(0, MODES)
    def _(plane):
        weight[...] += mine[plane] * mine[plane] + theirs[plane] * theirs[plane]

    @pl.loop(0, 3)
    def _(slot):
        here, top_row, offset = window_of(pos_ref, tiles, slot)

        @pl.when(here)
        def _():
            base, extra = aligned(top_row)
            ratio[...] = power[slot]
            sides = (patch.at[slot, 0], patch.at[slot, 1])
            forward(theirs, (0, 1), *sides, stacks, low, midb, far_too.at[0:2], ratio)
            forward(theirs, (2, 3), *sides, stacks, low, midb, far_too.at[2:4], ratio)
            ratio[...] = jnp.sqrt(meas[slot]) / jnp.sqrt(ratio[...] + 1.0)
            acc[0] = -weight[...] * patch[slot, 0]
            acc[1] = -weight[...] * patch[slot, 1]
            fields = [(far.at[slot, i], mine, i) for i in range(HELD)]
            fields += [(far_too.at[i], theirs, i) for i in range(HELD)]
            for start in range(0, MODES, GROUP):
                group = fields[start : start + GROUP]
                for unit, (source, _, _) in enumerate(group):
                    own = columns_of(unit)
                    low[:P_SIZE, own] = (source[:, :P_SIZE] * ratio[...]).astype(BF16)
                    low[P_SIZE:, own] = (source[:, P_SIZE:] * ratio[...]).astype(BF16)
                out = mix(stacks[1], stacks[0], low, midb, GROUP)
                term_re = 0.0
                term_im = 0.0
                for unit, (_, probe, mode) in enumerate(group):
                    back_re = out[columns_of(unit), :P_SIZE]
                    back_im = out[columns_of(unit), P_SIZE:]
                    pr = probe[2 * mode]
                    pi = probe[2 * mode + 1]
                    term_re += pr * back_re + pi * back_im
                    term_im += pr * back_im - pi * back_re
                acc[0] += term_re
                acc[1] += term_im

            for part in range(2):
                total[part, pl.ds(base, TALL), :] += pltpu.roll(lowered(acc[part], extra, EXT), offset, 1)

    mid_out[...] = total[:, :OH, pl.ds(pl.multiple_of(core * HALF, HALF), TW)]
    rim_out[...] = total[:, :OH, pl.ds(pl.multiple_of((1 - core) * TW, HALF), HALF)]


def denom_kernel(tiles, pos_ref, weight, scale, denom):
    tile, _ = place_of(tiles)
    denom[...] = jnp.zeros_like(denom)
    for parity, shifts in ((0, (-2, -1, 0, 1)), (1, (-1, 0, 1, 2))):
        for shift in shifts:
            inside, top_row, column = slot_of(pos_ref, tile, parity, tiles, shift)
            start = column - HALF - tile * TW

            @pl.when(inside & (start > -P_SIZE) & (start < TW))
            def _():
                base, extra = aligned(top_row)
                wide = lowered(weight[...], extra, 2 * P_SIZE)
                turned = pltpu.roll(wide, jnp.where(start < 0, start + 2 * P_SIZE, start), 1)
                denom[pl.ds(base, TALL), :] += turned[:, :TW]

    scale[...] = 1.0 / (denom[:OH] + 0.5)


ANY = pl.BlockSpec(memory_space=pl.ANY)
HBM = pl.BlockSpec(memory_space=pltpu.HBM)
VMEM = pl.BlockSpec(memory_space=pltpu.VMEM)
SMEM = pl.BlockSpec(memory_space=pltpu.SMEM)


def f32(*shape):
    return jax.ShapeDtypeStruct(shape, F32)


def limit(mib):
    return pltpu.CompilerParams(vmem_limit_bytes=mib * 2**20)


def cost(us):
    return pl.CostEstimate(flops=0, bytes_accessed=int(us * 3.5e6), transcendentals=0)


def local(intensity, positions, object_field, probe_modes, kernel_taps):
    tiles = lax.axis_size("tile")
    modes = lax.axis_size("mode")
    core = lax.rem(lax.axis_index("mode"), 2)
    spots = positions.T

    def along_x(array, steps):
        return lax.ppermute(array, "mode", [(i, (i + 2 * steps) % modes) for i in range(modes)])

    def swap(array):
        return lax.ppermute(array, "mode", [(i, i ^ 1) for i in range(modes)])

    def from_tile(array, step):
        pairs = []
        for tile in range(tiles):
            for mode in range(modes):
                source = tile + step if mode % 2 == 0 else tile - step
                if 0 <= source < tiles:
                    pairs.append((source * modes + mode, tile * modes + mode))
        return lax.ppermute(array, ("tile", "mode"), pairs)

    ring = [along_x(probe_modes, step) for step in (1, -1, 2)]
    edge, held = pl.pallas_call(
        pack_kernel,
        out_shape=(f32(2, OH, HALF), f32(MODES + 1, P_SIZE, P_SIZE)),
        in_specs=[ANY, ANY],
        out_specs=(VMEM, VMEM),
        scratch_shapes=[pltpu.SemaphoreType.DMA((2,))],
        compiler_params=limit(4),
        cost_estimate=cost(2.2),
        name="pack",
    )(object_field, probe_modes)
    beside = from_tile(edge, 1)
    inward = from_tile(intensity, 1)

    def stages(units):
        return [
            pltpu.VMEM((2 * P_SIZE, units * P_SIZE), BF16),
            pltpu.VMEM((units * P_SIZE, 2 * P_SIZE), BF16),
        ]

    mine = pl.pallas_call(
        merge_kernel,
        out_shape=f32(MODES + 1, P_SIZE, P_SIZE),
        in_specs=[ANY] * 4,
        out_specs=ANY,
        scratch_shapes=[pltpu.SemaphoreType.DMA((3,))],
        input_output_aliases={0: 0},
        compiler_params=limit(4),
        cost_estimate=cost(1.0),
        name="merge",
    )(held, *ring)
    mine = pl.pallas_call(
        append_kernel,
        out_shape=f32(MODES + 1, P_SIZE, P_SIZE),
        in_specs=[ANY, ANY],
        out_specs=ANY,
        scratch_shapes=[pltpu.SemaphoreType.DMA((1,))],
        input_output_aliases={1: 0},
        compiler_params=limit(4),
        name="append",
    )(inward, mine)
    mine, beside = lax.optimization_barrier((mine, beside))
    theirs = swap(mine)

    patch, stacks, far, power = pl.pallas_call(
        functools.partial(first_kernel, tiles),
        out_shape=(
            f32(3, 2, P_SIZE, P_SIZE),
            jax.ShapeDtypeStruct((2, 2 * P_SIZE, 2 * P_SIZE), BF16),
            f32(3, HELD, P_SIZE, 2 * P_SIZE),
            f32(3, P_SIZE, P_SIZE),
        ),
        in_specs=[SMEM, VMEM, ANY, ANY, VMEM],
        out_specs=(VMEM,) * 4,
        scratch_shapes=[pltpu.VMEM((2, OH + 8, EXT), F32)]
        + stages(GROUP)
        + [pltpu.VMEM((8, 2 * P_SIZE), F32), pltpu.SemaphoreType.DMA((2,))],
        compiler_params=limit(16),
        cost_estimate=cost(6.0),
        name="far_of_own_modes",
    )(spots, kernel_taps, object_field, beside, mine)

    middle, rim, weight = pl.pallas_call(
        functools.partial(second_kernel, tiles),
        out_shape=(f32(2, OH, TW), f32(2, OH, HALF), f32(P_SIZE, P_SIZE)),
        in_specs=[SMEM] + [VMEM] * 8,
        out_specs=(VMEM,) * 3,
        scratch_shapes=[
            pltpu.VMEM((2, OH + 8, EXT), F32),
            pltpu.VMEM((3, P_SIZE, P_SIZE), F32),
            pltpu.VMEM((HELD, P_SIZE, 2 * P_SIZE), F32),
        ]
        + stages(GROUP)
        + [pltpu.VMEM((P_SIZE, P_SIZE), F32), pltpu.VMEM((2, P_SIZE, P_SIZE), F32)],
        compiler_params=limit(20),
        cost_estimate=cost(10.0),
        name="update_terms",
    )(spots, intensity, inward, mine, theirs, far, patch, power, stacks)

    arrived = from_tile(rim, -1)
    scale = pl.pallas_call(
        functools.partial(denom_kernel, tiles),
        out_shape=f32(OH, TW),
        in_specs=[SMEM, VMEM],
        out_specs=VMEM,
        scratch_shapes=[pltpu.VMEM((OH + 8, TW), F32)],
        compiler_params=limit(4),
        cost_estimate=cost(3.5),
        name="denominator",
    )(spots, weight)
    blank = jnp.zeros_like(arrived)
    low = jnp.where(core == 0, arrived, blank)
    high = jnp.where(core == 0, blank, arrived)
    terms = (middle + jnp.concatenate([low, high], axis=2)) * scale
    return object_field + (terms + swap(terms))


def solution(mesh):
    return jax.shard_map(
        local,
        mesh=mesh,
        in_specs=(
            P("tile", None, None),
            P(),
            P(None, None, "tile"),
            P("mode", None, None, None),
            P(),
        ),
        out_specs=P(None, None, "tile"),
        check_vma=False,
    )
```

```python
import functools

import jax
import jax.numpy as jnp
from jax import lax
from jax.experimental import pallas as pl
from jax.experimental.pallas import tpu as pltpu
from jax.sharding import PartitionSpec as P

P_SIZE = 256
BAND = 64
TW = 256
HALF = 128
OH = 320
MODES = 8
EXT = TW + HALF
TALL = P_SIZE + 8
GROUP = 2
HELD = MODES // 2
F32 = jnp.float32
BF16 = jnp.bfloat16


def place_of(tiles):
    return lax.axis_index("tile"), lax.rem(lax.axis_index("mode"), 2)


def slot_of(pos_ref, tile, core, tiles, shift):
    block = tile + shift
    inside = (block >= 0) & (block < tiles)
    pattern = 2 * jnp.clip(block, 0, tiles - 1) + core
    return inside, pos_ref[0, pattern], pos_ref[1, pattern]


def aligned(top_row):
    extra = lax.rem(top_row, 8)
    return pl.multiple_of(top_row - extra, 8), extra


def lowered(window, extra, width):
    tall = jnp.concatenate([window, jnp.zeros((TALL - P_SIZE, P_SIZE), F32)], axis=0)
    return jnp.concatenate([pltpu.roll(tall, extra, 0), jnp.zeros((TALL, width - P_SIZE), F32)], axis=1)


def run_copies(moves, sem):
    copies = [pltpu.make_async_copy(src, dst, sem.at[i]) for i, (src, dst) in enumerate(moves)]
    for copy in copies:
        copy.start()
    for copy in copies:
        copy.wait()


def pack_kernel(obj, own, halo, merged, sem):
    core = lax.rem(lax.axis_index("mode"), 2)
    edge = pl.ds(pl.multiple_of(core * HALF, HALF), HALF)
    run_copies([(obj.at[:, :, edge], halo), (own.at[0], merged.at[0:2])], sem)


def merge_kernel(before, first, second, third, merged, sem):
    del before
    arrays = (first, second, third)
    run_copies([(array.at[0], merged.at[2 * i + 2 : 2 * i + 4]) for i, array in enumerate(arrays)], sem)


def append_kernel(inward, before, merged, sem):
    del before
    core = lax.rem(lax.axis_index("mode"), 2)
    run_copies([(inward.at[1 - core], merged.at[MODES])], sem)


def window_of(pos_ref, tiles, slot):
    tile, core = place_of(tiles)
    inside, top_row, column = slot_of(pos_ref, tile, core, tiles, (slot - 1) * (1 - 2 * core))
    offset = column - tile * TW - (1 - core) * HALF
    here = inside & (column >= tile * TW) & (column < (tile + 1) * TW)
    return here, top_row, offset


def columns_of(unit):
    return slice(unit * P_SIZE, (unit + 1) * P_SIZE)


def mix(first, second, low, midb, units):
    width = units * P_SIZE
    mid = jnp.dot(first, low[:, :width], preferred_element_type=F32)
    for unit in range(units):
        own = columns_of(unit)
        midb[own, :P_SIZE] = mid[:P_SIZE, own].astype(BF16)
        midb[own, P_SIZE:] = mid[P_SIZE:, own].astype(BF16)
    return jnp.dot(midb[:width], second, preferred_element_type=F32)


def forward(probe, modes, patch_re, patch_im, stacks, low, midb, far, power):
    for unit, mode in enumerate(modes):
        own = columns_of(unit)
        pr = probe[2 * mode]
        pi = probe[2 * mode + 1]
        low[:P_SIZE, own] = (pr * patch_re[...] - pi * patch_im[...]).astype(BF16)
        low[P_SIZE:, own] = (pr * patch_im[...] + pi * patch_re[...]).astype(BF16)
    out = mix(stacks[0], stacks[1], low, midb, len(modes))
    for unit in range(len(modes)):
        block = out[columns_of(unit)]
        far[unit] = block
        power[...] += block[:, :P_SIZE] * block[:, :P_SIZE] + block[:, P_SIZE:] * block[:, P_SIZE:]


def first_kernel(tiles, pos_ref, taps_ref, obj, beside, mine, patch, stacks, far, power, wave, low, midb, row_pad, sem):
    _, core = place_of(tiles)
    rim = pl.ds(pl.multiple_of((1 - core) * TW, HALF), HALF)
    moves = (
        (obj, wave.at[:, :OH, pl.ds(pl.multiple_of(core * HALF, HALF), TW)]),
        (beside, wave.at[:, :OH, rim]),
    )
    copies = [pltpu.make_async_copy(src, dst, sem.at[i]) for i, (src, dst) in enumerate(moves)]
    for copy in copies:
        copy.start()

    row_pad[...] = jnp.zeros_like(row_pad)
    row_pad[0:2, 0 : 2 * BAND + 1] = taps_ref[...]

    def band(part):
        line = jnp.broadcast_to(row_pad[part : part + 1, :], (P_SIZE, 2 * P_SIZE))
        turned = pltpu.roll(line, 2 * P_SIZE - BAND, 1, stride=1, stride_axis=0)
        return turned[:, :P_SIZE]

    band_re = band(0)
    band_im = band(1)
    turned_re = band_re.T
    turned_im = band_im.T
    for which, blocks in enumerate(((band_re, -band_im, band_im), (turned_re, turned_im, -turned_im))):
        stacks[which, :P_SIZE, :P_SIZE] = blocks[0].astype(BF16)
        stacks[which, :P_SIZE, P_SIZE:] = blocks[1].astype(BF16)
        stacks[which, P_SIZE:, :P_SIZE] = blocks[2].astype(BF16)
        stacks[which, P_SIZE:, P_SIZE:] = blocks[0].astype(BF16)

    for copy in copies:
        copy.wait()

    @pl.loop(0, 3)
    def _(slot):
        here, top_row, offset = window_of(pos_ref, tiles, slot)

        @pl.when(here)
        def _():
            base, extra = aligned(top_row)
            for part in range(2):
                rows = wave[part, pl.ds(base, TALL), :]
                turned = pltpu.roll(rows, lax.rem(EXT - offset, EXT), 1)[:, :P_SIZE]
                patch[slot, part] = pltpu.roll(turned, lax.rem(TALL - extra, TALL), 0)[:P_SIZE]
            power[slot] = jnp.zeros((P_SIZE, P_SIZE), F32)
            sides = (patch.at[slot, 0], patch.at[slot, 1])
            forward(mine, (0, 1), *sides, stacks, low, midb, far.at[slot, 0:2], power.at[slot])
            forward(mine, (2, 3), *sides, stacks, low, midb, far.at[slot, 2:4], power.at[slot])


def second_kernel(
    tiles, pos_ref, inten, inward, mine, theirs, far, patch, power, stacks, mid_out, rim_out, weight,
    total, meas, far_too, low, midb, ratio, acc,
):
    _, core = place_of(tiles)
    total[...] = jnp.zeros_like(total)
    meas[0] = theirs[MODES]
    meas[1] = inten[core]
    meas[2] = inward[core]
    weight[...] = jnp.zeros_like(weight)

    @pl.loop(0, MODES)
    def _(plane):
        weight[...] += mine[plane] * mine[plane] + theirs[plane] * theirs[plane]

    @pl.loop(0, 3)
    def _(slot):
        here, top_row, offset = window_of(pos_ref, tiles, slot)

        @pl.when(here)
        def _():
            base, extra = aligned(top_row)
            ratio[...] = power[slot]
            sides = (patch.at[slot, 0], patch.at[slot, 1])
            forward(theirs, (0, 1), *sides, stacks, low, midb, far_too.at[0:2], ratio)
            forward(theirs, (2, 3), *sides, stacks, low, midb, far_too.at[2:4], ratio)
            ratio[...] = jnp.sqrt(meas[slot]) / jnp.sqrt(ratio[...] + 1.0)
            acc[0] = -weight[...] * patch[slot, 0]
            acc[1] = -weight[...] * patch[slot, 1]
            fields = [(far.at[slot, i], mine, i) for i in range(HELD)]
            fields += [(far_too.at[i], theirs, i) for i in range(HELD)]
            for start in range(0, MODES, GROUP):
                group = fields[start : start + GROUP]
                for unit, (source, _, _) in enumerate(group):
                    own = columns_of(unit)
                    low[:P_SIZE, own] = (source[:, :P_SIZE] * ratio[...]).astype(BF16)
                    low[P_SIZE:, own] = (source[:, P_SIZE:] * ratio[...]).astype(BF16)
                out = mix(stacks[1], stacks[0], low, midb, GROUP)
                term_re = 0.0
                term_im = 0.0
                for unit, (_, probe, mode) in enumerate(group):
                    back_re = out[columns_of(unit), :P_SIZE]
                    back_im = out[columns_of(unit), P_SIZE:]
                    pr = probe[2 * mode]
                    pi = probe[2 * mode + 1]
                    term_re += pr * back_re + pi * back_im
                    term_im += pr * back_im - pi * back_re
                acc[0] += term_re
                acc[1] += term_im

            for part in range(2):
                total[part, pl.ds(base, TALL), :] += pltpu.roll(lowered(acc[part], extra, EXT), offset, 1)

    mid_out[...] = total[:, :OH, pl.ds(pl.multiple_of(core * HALF, HALF), TW)]
    rim_out[...] = total[:, :OH, pl.ds(pl.multiple_of((1 - core) * TW, HALF), HALF)]


def denom_kernel(tiles, pos_ref, weight, scale, denom):
    tile, _ = place_of(tiles)
    denom[...] = jnp.zeros_like(denom)
    for parity, shifts in ((0, (-2, -1, 0, 1)), (1, (-1, 0, 1, 2))):
        for shift in shifts:
            inside, top_row, column = slot_of(pos_ref, tile, parity, tiles, shift)
            start = column - HALF - tile * TW

            @pl.when(inside & (start > -P_SIZE) & (start < TW))
            def _():
                base, extra = aligned(top_row)
                wide = lowered(weight[...], extra, 2 * P_SIZE)
                turned = pltpu.roll(wide, jnp.where(start < 0, start + 2 * P_SIZE, start), 1)
                denom[pl.ds(base, TALL), :] += turned[:, :TW]

    scale[...] = 1.0 / (denom[:OH] + 0.5)


ANY = pl.BlockSpec(memory_space=pl.ANY)
HBM = pl.BlockSpec(memory_space=pltpu.HBM)
VMEM = pl.BlockSpec(memory_space=pltpu.VMEM)
SMEM = pl.BlockSpec(memory_space=pltpu.SMEM)


def f32(*shape):
    return jax.ShapeDtypeStruct(shape, F32)


def limit(mib):
    return pltpu.CompilerParams(vmem_limit_bytes=mib * 2**20)


def cost(us):
    return pl.CostEstimate(flops=0, bytes_accessed=int(us * 3.5e6), transcendentals=0)


def local(intensity, positions, object_field, probe_modes, kernel_taps):
    tiles = lax.axis_size("tile")
    modes = lax.axis_size("mode")
    core = lax.rem(lax.axis_index("mode"), 2)
    spots = positions.T

    def along_x(array, steps):
        return lax.ppermute(array, "mode", [(i, (i + 2 * steps) % modes) for i in range(modes)])

    def swap(array):
        return lax.ppermute(array, "mode", [(i, i ^ 1) for i in range(modes)])

    def from_tile(array, step):
        pairs = []
        for tile in range(tiles):
            for mode in range(modes):
                source = tile + step if mode % 2 == 0 else tile - step
                if 0 <= source < tiles:
                    pairs.append((source * modes + mode, tile * modes + mode))
        return lax.ppermute(array, ("tile", "mode"), pairs)

    ring = [along_x(probe_modes, step) for step in (2, 1, -1)]
    edge, held = pl.pallas_call(
        pack_kernel,
        out_shape=(f32(2, OH, HALF), f32(MODES + 1, P_SIZE, P_SIZE)),
        in_specs=[ANY, ANY],
        out_specs=(VMEM, VMEM),
        scratch_shapes=[pltpu.SemaphoreType.DMA((2,))],
        compiler_params=limit(4),
        cost_estimate=cost(2.2),
        name="pack",
    )(object_field, probe_modes)
    beside = from_tile(edge, 1)
    inward = from_tile(intensity, 1)

    def stages(units):
        return [
            pltpu.VMEM((2 * P_SIZE, units * P_SIZE), BF16),
            pltpu.VMEM((units * P_SIZE, 2 * P_SIZE), BF16),
        ]

    mine = pl.pallas_call(
        merge_kernel,
        out_shape=f32(MODES + 1, P_SIZE, P_SIZE),
        in_specs=[ANY] * 4,
        out_specs=ANY,
        scratch_shapes=[pltpu.SemaphoreType.DMA((3,))],
        input_output_aliases={0: 0},
        compiler_params=limit(4),
        cost_estimate=cost(1.0),
        name="merge",
    )(held, *ring)
    mine = pl.pallas_call(
        append_kernel,
        out_shape=f32(MODES + 1, P_SIZE, P_SIZE),
        in_specs=[ANY, ANY],
        out_specs=ANY,
        scratch_shapes=[pltpu.SemaphoreType.DMA((1,))],
        input_output_aliases={1: 0},
        compiler_params=limit(4),
        name="append",
    )(inward, mine)
    mine, beside = lax.optimization_barrier((mine, beside))
    theirs = swap(mine)

    patch, stacks, far, power = pl.pallas_call(
        functools.partial(first_kernel, tiles),
        out_shape=(
            f32(3, 2, P_SIZE, P_SIZE),
            jax.ShapeDtypeStruct((2, 2 * P_SIZE, 2 * P_SIZE), BF16),
            f32(3, HELD, P_SIZE, 2 * P_SIZE),
            f32(3, P_SIZE, P_SIZE),
        ),
        in_specs=[SMEM, VMEM, ANY, ANY, VMEM],
        out_specs=(VMEM,) * 4,
        scratch_shapes=[pltpu.VMEM((2, OH + 8, EXT), F32)]
        + stages(GROUP)
        + [pltpu.VMEM((8, 2 * P_SIZE), F32), pltpu.SemaphoreType.DMA((2,))],
        compiler_params=limit(16),
        cost_estimate=cost(6.0),
        name="far_of_own_modes",
    )(spots, kernel_taps, object_field, beside, mine)

    middle, rim, weight = pl.pallas_call(
        functools.partial(second_kernel, tiles),
        out_shape=(f32(2, OH, TW), f32(2, OH, HALF), f32(P_SIZE, P_SIZE)),
        in_specs=[SMEM] + [VMEM] * 8,
        out_specs=(VMEM,) * 3,
        scratch_shapes=[
            pltpu.VMEM((2, OH + 8, EXT), F32),
            pltpu.VMEM((3, P_SIZE, P_SIZE), F32),
            pltpu.VMEM((HELD, P_SIZE, 2 * P_SIZE), F32),
        ]
        + stages(GROUP)
        + [pltpu.VMEM((P_SIZE, P_SIZE), F32), pltpu.VMEM((2, P_SIZE, P_SIZE), F32)],
        compiler_params=limit(20),
        cost_estimate=cost(10.0),
        name="update_terms",
    )(spots, intensity, inward, mine, theirs, far, patch, power, stacks)

    arrived = from_tile(rim, -1)
    scale = pl.pallas_call(
        functools.partial(denom_kernel, tiles),
        out_shape=f32(OH, TW),
        in_specs=[SMEM, VMEM],
        out_specs=VMEM,
        scratch_shapes=[pltpu.VMEM((OH + 8, TW), F32)],
        compiler_params=limit(4),
        cost_estimate=cost(3.5),
        name="denominator",
    )(spots, weight)
    blank = jnp.zeros_like(arrived)
    low = jnp.where(core == 0, arrived, blank)
    high = jnp.where(core == 0, blank, arrived)
    terms = (middle + jnp.concatenate([low, high], axis=2)) * scale
    return object_field + (terms + swap(terms))


def solution(mesh):
    return jax.shard_map(
        local,
        mesh=mesh,
        in_specs=(
            P("tile", None, None),
            P(),
            P(None, None, "tile"),
            P("mode", None, None, None),
            P(),
        ),
        out_specs=P(None, None, "tile"),
        check_vma=False,
    )
```

```python
import functools

import jax
import jax.numpy as jnp
from jax import lax
from jax.experimental import pallas as pl
from jax.experimental.pallas import tpu as pltpu
from jax.sharding import PartitionSpec as P

P_SIZE = 256
BAND = 64
TW = 256
HALF = 128
OH = 320
MODES = 8
EXT = TW + HALF
TALL = P_SIZE + 8
GROUP = 2
HELD = MODES // 2
REACH = P_SIZE - BAND
F32 = jnp.float32
BF16 = jnp.bfloat16


def place_of(tiles):
    return lax.axis_index("tile"), lax.rem(lax.axis_index("mode"), 2)


def slot_of(pos_ref, tile, core, tiles, shift):
    block = tile + shift
    inside = (block >= 0) & (block < tiles)
    pattern = 2 * jnp.clip(block, 0, tiles - 1) + core
    return inside, pos_ref[0, pattern], pos_ref[1, pattern]


def aligned(top_row):
    extra = lax.rem(top_row, 8)
    return pl.multiple_of(top_row - extra, 8), extra


def lowered(window, extra, width):
    tall = jnp.concatenate([window, jnp.zeros((TALL - P_SIZE, P_SIZE), F32)], axis=0)
    return jnp.concatenate([pltpu.roll(tall, extra, 0), jnp.zeros((TALL, width - P_SIZE), F32)], axis=1)


def run_copies(moves, sem):
    copies = [pltpu.make_async_copy(src, dst, sem.at[i]) for i, (src, dst) in enumerate(moves)]
    for copy in copies:
        copy.start()
    for copy in copies:
        copy.wait()


def pack_kernel(obj, own, halo, merged, sem):
    core = lax.rem(lax.axis_index("mode"), 2)
    edge = pl.ds(pl.multiple_of(core * HALF, HALF), HALF)
    run_copies([(obj.at[:, :, edge], halo), (own.at[0], merged.at[0:2])], sem)


def merge_kernel(before, first, second, third, merged, sem):
    del before
    arrays = (first, second, third)
    run_copies([(array.at[0], merged.at[2 * i + 2 : 2 * i + 4]) for i, array in enumerate(arrays)], sem)


def append_kernel(inward, before, merged, sem):
    del before
    core = lax.rem(lax.axis_index("mode"), 2)
    run_copies([(inward.at[1 - core], merged.at[MODES])], sem)


def window_of(pos_ref, tiles, slot):
    tile, core = place_of(tiles)
    inside, top_row, column = slot_of(pos_ref, tile, core, tiles, (slot - 1) * (1 - 2 * core))
    offset = column - tile * TW - (1 - core) * HALF
    here = inside & (column >= tile * TW) & (column < (tile + 1) * TW)
    return here, top_row, offset


def columns_of(unit):
    return slice(unit * P_SIZE, (unit + 1) * P_SIZE)


def put_split(low, own, value_re, value_im):
    low[:HALF, own] = value_re[:HALF].astype(BF16)
    low[HALF : 2 * HALF, own] = value_im[:HALF].astype(BF16)
    low[2 * HALF : 3 * HALF, own] = value_re[HALF:].astype(BF16)
    low[3 * HALF :, own] = value_im[HALF:].astype(BF16)


def mix(left, second, low, midb):
    upper = jnp.dot(left[0], low[: 2 * HALF], preferred_element_type=F32)
    lower = jnp.dot(left[1], low[2 * HALF :], preferred_element_type=F32)
    for unit in range(GROUP):
        own = columns_of(unit)
        first_row = unit * P_SIZE
        for part in range(2):
            to = slice(part * P_SIZE, (part + 1) * P_SIZE)
            up = upper[part * REACH : (part + 1) * REACH, own]
            down = lower[part * REACH : (part + 1) * REACH, own]
            midb[first_row : first_row + BAND, to] = up[:BAND].astype(BF16)
            midb[first_row + BAND : first_row + REACH, to] = (up[BAND:] + down[: REACH - BAND]).astype(BF16)
            midb[first_row + REACH : first_row + P_SIZE, to] = down[REACH - BAND :].astype(BF16)
    return jnp.dot(midb[...], second, preferred_element_type=F32)


def forward(probe, modes, patch_re, patch_im, left, stacks, low, midb, far, power):
    for unit, mode in enumerate(modes):
        pr = probe[2 * mode]
        pi = probe[2 * mode + 1]
        re, im = patch_re[...], patch_im[...]
        put_split(low, columns_of(unit), pr * re - pi * im, pr * im + pi * re)
    out = mix(left.at[0], stacks[1], low, midb)
    for unit in range(len(modes)):
        block = out[columns_of(unit)]
        far[unit] = block
        power[...] += block[:, :P_SIZE] * block[:, :P_SIZE] + block[:, P_SIZE:] * block[:, P_SIZE:]


def first_kernel(tiles, pos_ref, taps_ref, obj, beside, mine, patch, left, stacks, far, power, wave, low, midb, row_pad, sem):
    _, core = place_of(tiles)
    rim = pl.ds(pl.multiple_of((1 - core) * TW, HALF), HALF)
    moves = (
        (obj, wave.at[:, :OH, pl.ds(pl.multiple_of(core * HALF, HALF), TW)]),
        (beside, wave.at[:, :OH, rim]),
    )
    copies = [pltpu.make_async_copy(src, dst, sem.at[i]) for i, (src, dst) in enumerate(moves)]
    for copy in copies:
        copy.start()

    row_pad[...] = jnp.zeros_like(row_pad)
    row_pad[0:2, 0 : 2 * BAND + 1] = taps_ref[...]

    def band(part):
        line = jnp.broadcast_to(row_pad[part : part + 1, :], (P_SIZE, 2 * P_SIZE))
        turned = pltpu.roll(line, 2 * P_SIZE - BAND, 1, stride=1, stride_axis=0)
        return turned[:, :P_SIZE]

    band_re = band(0)
    band_im = band(1)
    turned_re = band_re.T
    turned_im = band_im.T
    for which, blocks in enumerate(((band_re, -band_im, band_im), (turned_re, turned_im, -turned_im))):
        stacks[which, :P_SIZE, :P_SIZE] = blocks[0].astype(BF16)
        stacks[which, :P_SIZE, P_SIZE:] = blocks[1].astype(BF16)
        stacks[which, P_SIZE:, :P_SIZE] = blocks[2].astype(BF16)
        stacks[which, P_SIZE:, P_SIZE:] = blocks[0].astype(BF16)
        for half in range(2):
            rows = slice(half * BAND, half * BAND + REACH)
            part = slice(half * HALF, (half + 1) * HALF)
            left[which, half, :REACH, :HALF] = blocks[0][rows, part].astype(BF16)
            left[which, half, :REACH, HALF:] = blocks[1][rows, part].astype(BF16)
            left[which, half, REACH:, :HALF] = blocks[2][rows, part].astype(BF16)
            left[which, half, REACH:, HALF:] = blocks[0][rows, part].astype(BF16)

    for copy in copies:
        copy.wait()

    @pl.loop(0, 3)
    def _(slot):
        here, top_row, offset = window_of(pos_ref, tiles, slot)

        @pl.when(here)
        def _():
            base, extra = aligned(top_row)
            for part in range(2):
                rows = wave[part, pl.ds(base, TALL), :]
                turned = pltpu.roll(rows, lax.rem(EXT - offset, EXT), 1)[:, :P_SIZE]
                patch[slot, part] = pltpu.roll(turned, lax.rem(TALL - extra, TALL), 0)[:P_SIZE]
            power[slot] = jnp.zeros((P_SIZE, P_SIZE), F32)
            sides = (patch.at[slot, 0], patch.at[slot, 1])
            for turn in range(2):
                modes = (2 * turn, 2 * turn + 1)
                buffers = (low.at[turn], midb.at[turn])
                forward(mine, modes, *sides, left, stacks, *buffers, far.at[slot, 2 * turn : 2 * turn + 2], power.at[slot])


def second_kernel(
    tiles, pos_ref, inten, inward, mine, theirs, far, patch, power, left, stacks, mid_out, rim_out, weight,
    total, meas, far_too, low, midb, ratio, acc,
):
    _, core = place_of(tiles)
    total[...] = jnp.zeros_like(total)
    meas[0] = theirs[MODES]
    meas[1] = inten[core]
    meas[2] = inward[core]
    weight[...] = jnp.zeros_like(weight)

    @pl.loop(0, MODES)
    def _(plane):
        weight[...] += mine[plane] * mine[plane] + theirs[plane] * theirs[plane]

    @pl.loop(0, 3)
    def _(slot):
        here, top_row, offset = window_of(pos_ref, tiles, slot)

        @pl.when(here)
        def _():
            base, extra = aligned(top_row)
            ratio[...] = power[slot]
            sides = (patch.at[slot, 0], patch.at[slot, 1])
            for turn in range(2):
                modes = (2 * turn, 2 * turn + 1)
                buffers = (low.at[turn], midb.at[turn])
                forward(theirs, modes, *sides, left, stacks, *buffers, far_too.at[2 * turn : 2 * turn + 2], ratio)
            ratio[...] = jnp.sqrt(meas[slot]) / jnp.sqrt(ratio[...] + 1.0)
            acc[0] = -weight[...] * patch[slot, 0]
            acc[1] = -weight[...] * patch[slot, 1]
            fields = [(far.at[slot, i], mine, i) for i in range(HELD)]
            fields += [(far_too.at[i], theirs, i) for i in range(HELD)]
            for start in range(0, MODES, GROUP):
                group = fields[start : start + GROUP]
                turn = start // GROUP % 2
                for unit, (source, _, _) in enumerate(group):
                    scaled = ratio[...]
                    put_split(low.at[turn], columns_of(unit), source[:, :P_SIZE] * scaled, source[:, P_SIZE:] * scaled)
                out = mix(left.at[1], stacks[0], low.at[turn], midb.at[turn])
                term_re = 0.0
                term_im = 0.0
                for unit, (_, probe, mode) in enumerate(group):
                    back_re = out[columns_of(unit), :P_SIZE]
                    back_im = out[columns_of(unit), P_SIZE:]
                    pr = probe[2 * mode]
                    pi = probe[2 * mode + 1]
                    term_re += pr * back_re + pi * back_im
                    term_im += pr * back_im - pi * back_re
                acc[0] += term_re
                acc[1] += term_im

            for part in range(2):
                total[part, pl.ds(base, TALL), :] += pltpu.roll(lowered(acc[part], extra, EXT), offset, 1)

    mid_out[...] = total[:, :OH, pl.ds(pl.multiple_of(core * HALF, HALF), TW)]
    rim_out[...] = total[:, :OH, pl.ds(pl.multiple_of((1 - core) * TW, HALF), HALF)]


def denom_kernel(tiles, pos_ref, weight, scale, denom):
    tile, _ = place_of(tiles)
    denom[...] = jnp.zeros_like(denom)
    for parity, shifts in ((0, (-2, -1, 0, 1)), (1, (-1, 0, 1, 2))):
        for shift in shifts:
            inside, top_row, column = slot_of(pos_ref, tile, parity, tiles, shift)
            start = column - HALF - tile * TW

            @pl.when(inside & (start > -P_SIZE) & (start < TW))
            def _():
                base, extra = aligned(top_row)
                wide = lowered(weight[...], extra, 2 * P_SIZE)
                turned = pltpu.roll(wide, jnp.where(start < 0, start + 2 * P_SIZE, start), 1)
                denom[pl.ds(base, TALL), :] += turned[:, :TW]

    scale[...] = 1.0 / (denom[:OH] + 0.5)


ANY = pl.BlockSpec(memory_space=pl.ANY)
HBM = pl.BlockSpec(memory_space=pltpu.HBM)
VMEM = pl.BlockSpec(memory_space=pltpu.VMEM)
SMEM = pl.BlockSpec(memory_space=pltpu.SMEM)


def f32(*shape):
    return jax.ShapeDtypeStruct(shape, F32)


def limit(mib):
    return pltpu.CompilerParams(vmem_limit_bytes=mib * 2**20)


def cost(us):
    return pl.CostEstimate(flops=0, bytes_accessed=int(us * 3.5e6), transcendentals=0)


def local(intensity, positions, object_field, probe_modes, kernel_taps):
    tiles = lax.axis_size("tile")
    modes = lax.axis_size("mode")
    core = lax.rem(lax.axis_index("mode"), 2)
    spots = positions.T

    def along_x(array, steps):
        return lax.ppermute(array, "mode", [(i, (i + 2 * steps) % modes) for i in range(modes)])

    def swap(array):
        return lax.ppermute(array, "mode", [(i, i ^ 1) for i in range(modes)])

    def from_tile(array, step):
        pairs = []
        for tile in range(tiles):
            for mode in range(modes):
                source = tile + step if mode % 2 == 0 else tile - step
                if 0 <= source < tiles:
                    pairs.append((source * modes + mode, tile * modes + mode))
        return lax.ppermute(array, ("tile", "mode"), pairs)

    ring = [along_x(probe_modes, step) for step in (2, 1, -1)]
    edge, held = pl.pallas_call(
        pack_kernel,
        out_shape=(f32(2, OH, HALF), f32(MODES + 1, P_SIZE, P_SIZE)),
        in_specs=[ANY, ANY],
        out_specs=(VMEM, VMEM),
        scratch_shapes=[pltpu.SemaphoreType.DMA((2,))],
        compiler_params=limit(4),
        cost_estimate=cost(2.2),
        name="pack",
    )(object_field, probe_modes)
    beside = from_tile(edge, 1)
    inward = from_tile(intensity, 1)

    def stages(units):
        return [
            pltpu.VMEM((2, 2 * P_SIZE, units * P_SIZE), BF16),
            pltpu.VMEM((2, units * P_SIZE, 2 * P_SIZE), BF16),
        ]

    mine = pl.pallas_call(
        merge_kernel,
        out_shape=f32(MODES + 1, P_SIZE, P_SIZE),
        in_specs=[ANY] * 4,
        out_specs=ANY,
        scratch_shapes=[pltpu.SemaphoreType.DMA((3,))],
        input_output_aliases={0: 0},
        compiler_params=limit(4),
        cost_estimate=cost(1.0),
        name="merge",
    )(held, *ring)
    mine = pl.pallas_call(
        append_kernel,
        out_shape=f32(MODES + 1, P_SIZE, P_SIZE),
        in_specs=[ANY, ANY],
        out_specs=ANY,
        scratch_shapes=[pltpu.SemaphoreType.DMA((1,))],
        input_output_aliases={1: 0},
        compiler_params=limit(4),
        name="append",
    )(inward, mine)
    mine, beside = lax.optimization_barrier((mine, beside))
    theirs = swap(mine)

    patch, left, stacks, far, power = pl.pallas_call(
        functools.partial(first_kernel, tiles),
        out_shape=(
            f32(3, 2, P_SIZE, P_SIZE),
            jax.ShapeDtypeStruct((2, 2, 2 * REACH, 2 * HALF), BF16),
            jax.ShapeDtypeStruct((2, 2 * P_SIZE, 2 * P_SIZE), BF16),
            f32(3, HELD, P_SIZE, 2 * P_SIZE),
            f32(3, P_SIZE, P_SIZE),
        ),
        in_specs=[SMEM, VMEM, ANY, ANY, VMEM],
        out_specs=(VMEM,) * 5,
        scratch_shapes=[pltpu.VMEM((2, OH + 8, EXT), F32)]
        + stages(GROUP)
        + [pltpu.VMEM((8, 2 * P_SIZE), F32), pltpu.SemaphoreType.DMA((2,))],
        compiler_params=limit(16),
        cost_estimate=cost(6.0),
        name="far_of_own_modes",
    )(spots, kernel_taps, object_field, beside, mine)

    middle, rim, weight = pl.pallas_call(
        functools.partial(second_kernel, tiles),
        out_shape=(f32(2, OH, TW), f32(2, OH, HALF), f32(P_SIZE, P_SIZE)),
        in_specs=[SMEM] + [VMEM] * 9,
        out_specs=(VMEM,) * 3,
        scratch_shapes=[
            pltpu.VMEM((2, OH + 8, EXT), F32),
            pltpu.VMEM((3, P_SIZE, P_SIZE), F32),
            pltpu.VMEM((HELD, P_SIZE, 2 * P_SIZE), F32),
        ]
        + stages(GROUP)
        + [pltpu.VMEM((P_SIZE, P_SIZE), F32), pltpu.VMEM((2, P_SIZE, P_SIZE), F32)],
        compiler_params=limit(20),
        cost_estimate=cost(10.0),
        name="update_terms",
    )(spots, intensity, inward, mine, theirs, far, patch, power, left, stacks)

    arrived = from_tile(rim, -1)
    scale = pl.pallas_call(
        functools.partial(denom_kernel, tiles),
        out_shape=f32(OH, TW),
        in_specs=[SMEM, VMEM],
        out_specs=VMEM,
        scratch_shapes=[pltpu.VMEM((OH + 8, TW), F32)],
        compiler_params=limit(4),
        cost_estimate=cost(3.5),
        name="denominator",
    )(spots, weight)
    blank = jnp.zeros_like(arrived)
    low = jnp.where(core == 0, arrived, blank)
    high = jnp.where(core == 0, blank, arrived)
    terms = (middle + jnp.concatenate([low, high], axis=2)) * scale
    return object_field + (terms + swap(terms))


def solution(mesh):
    return jax.shard_map(
        local,
        mesh=mesh,
        in_specs=(
            P("tile", None, None),
            P(),
            P(None, None, "tile"),
            P("mode", None, None, None),
            P(),
        ),
        out_specs=P(None, None, "tile"),
        check_vma=False,
    )
```

```python
import functools

import jax
import jax.numpy as jnp
from jax import lax
from jax.experimental import pallas as pl
from jax.experimental.pallas import tpu as pltpu
from jax.sharding import PartitionSpec as P

P_SIZE = 256
BAND = 64
TW = 256
HALF = 128
OH = 320
MODES = 8
EXT = TW + HALF
TALL = P_SIZE + 8
GROUP = 4
HELD = MODES // 2
REACH = P_SIZE - BAND
F32 = jnp.float32
BF16 = jnp.bfloat16


def place_of(tiles):
    return lax.axis_index("tile"), lax.rem(lax.axis_index("mode"), 2)


def slot_of(pos_ref, tile, core, tiles, shift):
    block = tile + shift
    inside = (block >= 0) & (block < tiles)
    pattern = 2 * jnp.clip(block, 0, tiles - 1) + core
    return inside, pos_ref[0, pattern], pos_ref[1, pattern]


def aligned(top_row):
    extra = lax.rem(top_row, 8)
    return pl.multiple_of(top_row - extra, 8), extra


def lowered(window, extra, width):
    tall = jnp.concatenate([window, jnp.zeros((TALL - P_SIZE, P_SIZE), F32)], axis=0)
    return jnp.concatenate([pltpu.roll(tall, extra, 0), jnp.zeros((TALL, width - P_SIZE), F32)], axis=1)


def run_copies(moves, sem):
    copies = [pltpu.make_async_copy(src, dst, sem.at[i]) for i, (src, dst) in enumerate(moves)]
    for copy in copies:
        copy.start()
    for copy in copies:
        copy.wait()


def pack_kernel(obj, own, halo, merged, sem):
    core = lax.rem(lax.axis_index("mode"), 2)
    edge = pl.ds(pl.multiple_of(core * HALF, HALF), HALF)
    run_copies([(obj.at[:, :, edge], halo), (own.at[0], merged.at[0:2])], sem)


def merge_kernel(before, first, second, third, merged, sem):
    del before
    arrays = (first, second, third)
    run_copies([(array.at[0], merged.at[2 * i + 2 : 2 * i + 4]) for i, array in enumerate(arrays)], sem)


def append_kernel(inward, before, merged, sem):
    del before
    core = lax.rem(lax.axis_index("mode"), 2)
    run_copies([(inward.at[1 - core], merged.at[MODES])], sem)


def window_of(pos_ref, tiles, slot):
    tile, core = place_of(tiles)
    inside, top_row, column = slot_of(pos_ref, tile, core, tiles, (slot - 1) * (1 - 2 * core))
    offset = column - tile * TW - (1 - core) * HALF
    here = inside & (column >= tile * TW) & (column < (tile + 1) * TW)
    return here, top_row, offset


def columns_of(unit):
    return slice(unit * P_SIZE, (unit + 1) * P_SIZE)


def put_split(low, own, value_re, value_im):
    low[:HALF, own] = value_re[:HALF].astype(BF16)
    low[HALF : 2 * HALF, own] = value_im[:HALF].astype(BF16)
    low[2 * HALF : 3 * HALF, own] = value_re[HALF:].astype(BF16)
    low[3 * HALF :, own] = value_im[HALF:].astype(BF16)


def mix(left, second, low, midb):
    upper = jnp.dot(left[0], low[: 2 * HALF], preferred_element_type=F32)
    lower = jnp.dot(left[1], low[2 * HALF :], preferred_element_type=F32)
    for unit in range(GROUP):
        own = columns_of(unit)
        first_row = unit * P_SIZE
        for part in range(2):
            to = slice(part * P_SIZE, (part + 1) * P_SIZE)
            up = upper[part * REACH : (part + 1) * REACH, own]
            down = lower[part * REACH : (part + 1) * REACH, own]
            midb[first_row : first_row + BAND, to] = up[:BAND].astype(BF16)
            midb[first_row + BAND : first_row + REACH, to] = (up[BAND:] + down[: REACH - BAND]).astype(BF16)
            midb[first_row + REACH : first_row + P_SIZE, to] = down[REACH - BAND :].astype(BF16)
    return jnp.dot(midb[...], second, preferred_element_type=F32)


def forward(probe, modes, patch_re, patch_im, left, stacks, low, midb, far, power):
    for unit, mode in enumerate(modes):
        pr = probe[2 * mode]
        pi = probe[2 * mode + 1]
        re, im = patch_re[...], patch_im[...]
        put_split(low, columns_of(unit), pr * re - pi * im, pr * im + pi * re)
    out = mix(left.at[0], stacks[1], low, midb)
    for unit in range(len(modes)):
        block = out[columns_of(unit)]
        far[unit] = block
        power[...] += block[:, :P_SIZE] * block[:, :P_SIZE] + block[:, P_SIZE:] * block[:, P_SIZE:]


def first_kernel(tiles, pos_ref, taps_ref, obj, beside, mine, patch, left, stacks, far, power, wave, low, midb, row_pad, sem):
    _, core = place_of(tiles)
    rim = pl.ds(pl.multiple_of((1 - core) * TW, HALF), HALF)
    moves = (
        (obj, wave.at[:, :OH, pl.ds(pl.multiple_of(core * HALF, HALF), TW)]),
        (beside, wave.at[:, :OH, rim]),
    )
    copies = [pltpu.make_async_copy(src, dst, sem.at[i]) for i, (src, dst) in enumerate(moves)]
    for copy in copies:
        copy.start()

    row_pad[...] = jnp.zeros_like(row_pad)
    row_pad[0:2, 0 : 2 * BAND + 1] = taps_ref[...]

    def band(part):
        line = jnp.broadcast_to(row_pad[part : part + 1, :], (P_SIZE, 2 * P_SIZE))
        turned = pltpu.roll(line, 2 * P_SIZE - BAND, 1, stride=1, stride_axis=0)
        return turned[:, :P_SIZE]

    band_re = band(0)
    band_im = band(1)
    turned_re = band_re.T
    turned_im = band_im.T
    for which, blocks in enumerate(((band_re, -band_im, band_im), (turned_re, turned_im, -turned_im))):
        stacks[which, :P_SIZE, :P_SIZE] = blocks[0].astype(BF16)
        stacks[which, :P_SIZE, P_SIZE:] = blocks[1].astype(BF16)
        stacks[which, P_SIZE:, :P_SIZE] = blocks[2].astype(BF16)
        stacks[which, P_SIZE:, P_SIZE:] = blocks[0].astype(BF16)
        for half in range(2):
            rows = slice(half * BAND, half * BAND + REACH)
            part = slice(half * HALF, (half + 1) * HALF)
            left[which, half, :REACH, :HALF] = blocks[0][rows, part].astype(BF16)
            left[which, half, :REACH, HALF:] = blocks[1][rows, part].astype(BF16)
            left[which, half, REACH:, :HALF] = blocks[2][rows, part].astype(BF16)
            left[which, half, REACH:, HALF:] = blocks[0][rows, part].astype(BF16)

    for copy in copies:
        copy.wait()

    @pl.loop(0, 3)
    def _(slot):
        here, top_row, offset = window_of(pos_ref, tiles, slot)

        @pl.when(here)
        def _():
            base, extra = aligned(top_row)
            for part in range(2):
                rows = wave[part, pl.ds(base, TALL), :]
                turned = pltpu.roll(rows, lax.rem(EXT - offset, EXT), 1)[:, :P_SIZE]
                patch[slot, part] = pltpu.roll(turned, lax.rem(TALL - extra, TALL), 0)[:P_SIZE]
            power[slot] = jnp.zeros((P_SIZE, P_SIZE), F32)
            sides = (patch.at[slot, 0], patch.at[slot, 1])
            forward(mine, range(GROUP), *sides, left, stacks, low.at[0], midb.at[0], far.at[slot], power.at[slot])


def second_kernel(
    tiles, pos_ref, inten, inward, mine, theirs, far, patch, power, left, stacks, mid_out, rim_out, weight,
    total, meas, far_too, low, midb, ratio, acc,
):
    _, core = place_of(tiles)
    total[...] = jnp.zeros_like(total)
    meas[0] = theirs[MODES]
    meas[1] = inten[core]
    meas[2] = inward[core]
    weight[...] = jnp.zeros_like(weight)

    @pl.loop(0, MODES)
    def _(plane):
        weight[...] += mine[plane] * mine[plane] + theirs[plane] * theirs[plane]

    @pl.loop(0, 3)
    def _(slot):
        here, top_row, offset = window_of(pos_ref, tiles, slot)

        @pl.when(here)
        def _():
            base, extra = aligned(top_row)
            ratio[...] = power[slot]
            sides = (patch.at[slot, 0], patch.at[slot, 1])
            forward(theirs, range(GROUP), *sides, left, stacks, low.at[0], midb.at[0], far_too, ratio)
            ratio[...] = jnp.sqrt(meas[slot]) / jnp.sqrt(ratio[...] + 1.0)
            acc[0] = -weight[...] * patch[slot, 0]
            acc[1] = -weight[...] * patch[slot, 1]
            fields = [(far.at[slot, i], mine, i) for i in range(HELD)]
            fields += [(far_too.at[i], theirs, i) for i in range(HELD)]
            for start in range(0, MODES, GROUP):
                group = fields[start : start + GROUP]
                turn = start // GROUP % 2
                for unit, (source, _, _) in enumerate(group):
                    scaled = ratio[...]
                    put_split(low.at[turn], columns_of(unit), source[:, :P_SIZE] * scaled, source[:, P_SIZE:] * scaled)
                out = mix(left.at[1], stacks[0], low.at[turn], midb.at[turn])
                term_re = 0.0
                term_im = 0.0
                for unit, (_, probe, mode) in enumerate(group):
                    back_re = out[columns_of(unit), :P_SIZE]
                    back_im = out[columns_of(unit), P_SIZE:]
                    pr = probe[2 * mode]
                    pi = probe[2 * mode + 1]
                    term_re += pr * back_re + pi * back_im
                    term_im += pr * back_im - pi * back_re
                acc[0] += term_re
                acc[1] += term_im

            for part in range(2):
                total[part, pl.ds(base, TALL), :] += pltpu.roll(lowered(acc[part], extra, EXT), offset, 1)

    mid_out[...] = total[:, :OH, pl.ds(pl.multiple_of(core * HALF, HALF), TW)]
    rim_out[...] = total[:, :OH, pl.ds(pl.multiple_of((1 - core) * TW, HALF), HALF)]


def denom_kernel(tiles, pos_ref, weight, scale, denom):
    tile, _ = place_of(tiles)
    denom[...] = jnp.zeros_like(denom)
    for parity, shifts in ((0, (-2, -1, 0, 1)), (1, (-1, 0, 1, 2))):
        for shift in shifts:
            inside, top_row, column = slot_of(pos_ref, tile, parity, tiles, shift)
            start = column - HALF - tile * TW

            @pl.when(inside & (start > -P_SIZE) & (start < TW))
            def _():
                base, extra = aligned(top_row)
                wide = lowered(weight[...], extra, 2 * P_SIZE)
                turned = pltpu.roll(wide, jnp.where(start < 0, start + 2 * P_SIZE, start), 1)
                denom[pl.ds(base, TALL), :] += turned[:, :TW]

    scale[...] = 1.0 / (denom[:OH] + 0.5)


ANY = pl.BlockSpec(memory_space=pl.ANY)
HBM = pl.BlockSpec(memory_space=pltpu.HBM)
VMEM = pl.BlockSpec(memory_space=pltpu.VMEM)
SMEM = pl.BlockSpec(memory_space=pltpu.SMEM)


def f32(*shape):
    return jax.ShapeDtypeStruct(shape, F32)


def limit(mib):
    return pltpu.CompilerParams(vmem_limit_bytes=mib * 2**20)


def cost(us):
    return pl.CostEstimate(flops=0, bytes_accessed=int(us * 3.5e6), transcendentals=0)


def local(intensity, positions, object_field, probe_modes, kernel_taps):
    tiles = lax.axis_size("tile")
    modes = lax.axis_size("mode")
    core = lax.rem(lax.axis_index("mode"), 2)
    spots = positions.T

    def along_x(array, steps):
        return lax.ppermute(array, "mode", [(i, (i + 2 * steps) % modes) for i in range(modes)])

    def swap(array):
        return lax.ppermute(array, "mode", [(i, i ^ 1) for i in range(modes)])

    def from_tile(array, step):
        pairs = []
        for tile in range(tiles):
            for mode in range(modes):
                source = tile + step if mode % 2 == 0 else tile - step
                if 0 <= source < tiles:
                    pairs.append((source * modes + mode, tile * modes + mode))
        return lax.ppermute(array, ("tile", "mode"), pairs)

    ring = [along_x(probe_modes, step) for step in (2, 1, -1)]
    edge, held = pl.pallas_call(
        pack_kernel,
        out_shape=(f32(2, OH, HALF), f32(MODES + 1, P_SIZE, P_SIZE)),
        in_specs=[ANY, ANY],
        out_specs=(VMEM, VMEM),
        scratch_shapes=[pltpu.SemaphoreType.DMA((2,))],
        compiler_params=limit(4),
        cost_estimate=cost(2.2),
        name="pack",
    )(object_field, probe_modes)
    beside = from_tile(edge, 1)
    inward = from_tile(intensity, 1)

    def stages(units):
        return [
            pltpu.VMEM((2, 2 * P_SIZE, units * P_SIZE), BF16),
            pltpu.VMEM((2, units * P_SIZE, 2 * P_SIZE), BF16),
        ]

    mine = pl.pallas_call(
        merge_kernel,
        out_shape=f32(MODES + 1, P_SIZE, P_SIZE),
        in_specs=[ANY] * 4,
        out_specs=ANY,
        scratch_shapes=[pltpu.SemaphoreType.DMA((3,))],
        input_output_aliases={0: 0},
        compiler_params=limit(4),
        cost_estimate=cost(1.0),
        name="merge",
    )(held, *ring)
    mine = pl.pallas_call(
        append_kernel,
        out_shape=f32(MODES + 1, P_SIZE, P_SIZE),
        in_specs=[ANY, ANY],
        out_specs=ANY,
        scratch_shapes=[pltpu.SemaphoreType.DMA((1,))],
        input_output_aliases={1: 0},
        compiler_params=limit(4),
        name="append",
    )(inward, mine)
    mine, beside = lax.optimization_barrier((mine, beside))
    theirs = swap(mine)

    patch, left, stacks, far, power = pl.pallas_call(
        functools.partial(first_kernel, tiles),
        out_shape=(
            f32(3, 2, P_SIZE, P_SIZE),
            jax.ShapeDtypeStruct((2, 2, 2 * REACH, 2 * HALF), BF16),
            jax.ShapeDtypeStruct((2, 2 * P_SIZE, 2 * P_SIZE), BF16),
            f32(3, HELD, P_SIZE, 2 * P_SIZE),
            f32(3, P_SIZE, P_SIZE),
        ),
        in_specs=[SMEM, VMEM, ANY, ANY, VMEM],
        out_specs=(VMEM,) * 5,
        scratch_shapes=[pltpu.VMEM((2, OH + 8, EXT), F32)]
        + stages(GROUP)
        + [pltpu.VMEM((8, 2 * P_SIZE), F32), pltpu.SemaphoreType.DMA((2,))],
        compiler_params=limit(16),
        cost_estimate=cost(6.0),
        name="far_of_own_modes",
    )(spots, kernel_taps, object_field, beside, mine)

    middle, rim, weight = pl.pallas_call(
        functools.partial(second_kernel, tiles),
        out_shape=(f32(2, OH, TW), f32(2, OH, HALF), f32(P_SIZE, P_SIZE)),
        in_specs=[SMEM] + [VMEM] * 9,
        out_specs=(VMEM,) * 3,
        scratch_shapes=[
            pltpu.VMEM((2, OH + 8, EXT), F32),
            pltpu.VMEM((3, P_SIZE, P_SIZE), F32),
            pltpu.VMEM((HELD, P_SIZE, 2 * P_SIZE), F32),
        ]
        + stages(GROUP)
        + [pltpu.VMEM((P_SIZE, P_SIZE), F32), pltpu.VMEM((2, P_SIZE, P_SIZE), F32)],
        compiler_params=limit(20),
        cost_estimate=cost(10.0),
        name="update_terms",
    )(spots, intensity, inward, mine, theirs, far, patch, power, left, stacks)

    arrived = from_tile(rim, -1)
    scale = pl.pallas_call(
        functools.partial(denom_kernel, tiles),
        out_shape=f32(OH, TW),
        in_specs=[SMEM, VMEM],
        out_specs=VMEM,
        scratch_shapes=[pltpu.VMEM((OH + 8, TW), F32)],
        compiler_params=limit(4),
        cost_estimate=cost(3.5),
        name="denominator",
    )(spots, weight)
    blank = jnp.zeros_like(arrived)
    low = jnp.where(core == 0, arrived, blank)
    high = jnp.where(core == 0, blank, arrived)
    terms = (middle + jnp.concatenate([low, high], axis=2)) * scale
    return object_field + (terms + swap(terms))


def solution(mesh):
    return jax.shard_map(
        local,
        mesh=mesh,
        in_specs=(
            P("tile", None, None),
            P(),
            P(None, None, "tile"),
            P("mode", None, None, None),
            P(),
        ),
        out_specs=P(None, None, "tile"),
        check_vma=False,
    )
```

```python
import functools

import jax
import jax.numpy as jnp
from jax import lax
from jax.experimental import pallas as pl
from jax.experimental.pallas import tpu as pltpu
from jax.sharding import PartitionSpec as P

P_SIZE = 256
BAND = 64
TW = 256
HALF = 128
OH = 320
MODES = 8
EXT = TW + HALF
TALL = P_SIZE + 8
GROUP = 4
HELD = MODES // 2
REACH = P_SIZE - BAND
F32 = jnp.float32
BF16 = jnp.bfloat16


def place_of(tiles):
    return lax.axis_index("tile"), lax.rem(lax.axis_index("mode"), 2)


def slot_of(pos_ref, tile, core, tiles, shift):
    block = tile + shift
    inside = (block >= 0) & (block < tiles)
    pattern = 2 * jnp.clip(block, 0, tiles - 1) + core
    return inside, pos_ref[0, pattern], pos_ref[1, pattern]


def aligned(top_row):
    extra = lax.rem(top_row, 8)
    return pl.multiple_of(top_row - extra, 8), extra


def lowered(window, extra, width):
    tall = jnp.concatenate([window, jnp.zeros((TALL - P_SIZE, P_SIZE), F32)], axis=0)
    return jnp.concatenate([pltpu.roll(tall, extra, 0), jnp.zeros((TALL, width - P_SIZE), F32)], axis=1)


def run_copies(moves, sem):
    copies = [pltpu.make_async_copy(src, dst, sem.at[i]) for i, (src, dst) in enumerate(moves)]
    for copy in copies:
        copy.start()
    for copy in copies:
        copy.wait()


def pack_kernel(obj, own, halo, merged, sem):
    core = lax.rem(lax.axis_index("mode"), 2)
    edge = pl.ds(pl.multiple_of(core * HALF, HALF), HALF)
    run_copies([(obj.at[:, :, edge], halo), (own.at[0], merged.at[0:2])], sem)


def merge_kernel(before, first, second, third, merged, sem):
    del before
    arrays = (first, second, third)
    run_copies([(array.at[0], merged.at[2 * i + 2 : 2 * i + 4]) for i, array in enumerate(arrays)], sem)


def append_kernel(inward, before, merged, sem):
    del before
    core = lax.rem(lax.axis_index("mode"), 2)
    run_copies([(inward.at[1 - core], merged.at[MODES])], sem)


def window_of(pos_ref, tiles, slot):
    tile, core = place_of(tiles)
    inside, top_row, column = slot_of(pos_ref, tile, core, tiles, (slot - 1) * (1 - 2 * core))
    offset = column - tile * TW - (1 - core) * HALF
    here = inside & (column >= tile * TW) & (column < (tile + 1) * TW)
    return here, top_row, offset


def columns_of(unit):
    return slice(unit * P_SIZE, (unit + 1) * P_SIZE)


def put_split(low, own, value_re, value_im):
    low[:HALF, own] = value_re[:HALF].astype(BF16)
    low[HALF : 2 * HALF, own] = value_im[:HALF].astype(BF16)
    low[2 * HALF : 3 * HALF, own] = value_re[HALF:].astype(BF16)
    low[3 * HALF :, own] = value_im[HALF:].astype(BF16)


def mix(left, second, low, midb):
    upper = jnp.dot(left[0], low[: 2 * HALF], preferred_element_type=F32)
    lower = jnp.dot(left[1], low[2 * HALF :], preferred_element_type=F32)
    for unit in range(GROUP):
        own = columns_of(unit)
        first_row = unit * P_SIZE
        for part in range(2):
            to = slice(part * P_SIZE, (part + 1) * P_SIZE)
            up = upper[part * REACH : (part + 1) * REACH, own]
            down = lower[part * REACH : (part + 1) * REACH, own]
            midb[first_row : first_row + BAND, to] = up[:BAND].astype(BF16)
            midb[first_row + BAND : first_row + REACH, to] = (up[BAND:] + down[: REACH - BAND]).astype(BF16)
            midb[first_row + REACH : first_row + P_SIZE, to] = down[REACH - BAND :].astype(BF16)
    return jnp.dot(midb[...], second, preferred_element_type=F32)


def forward(probe, modes, patch_re, patch_im, left, stacks, low, midb, far, power):
    for unit, mode in enumerate(modes):
        pr = probe[2 * mode]
        pi = probe[2 * mode + 1]
        re, im = patch_re[...], patch_im[...]
        put_split(low, columns_of(unit), pr * re - pi * im, pr * im + pi * re)
    out = mix(left.at[0], stacks[1], low, midb)
    for unit in range(len(modes)):
        block = out[columns_of(unit)]
        far[unit] = block
        power[...] += block[:, :P_SIZE] * block[:, :P_SIZE] + block[:, P_SIZE:] * block[:, P_SIZE:]


def first_kernel(tiles, pos_ref, taps_ref, obj, beside, mine, patch, left, stacks, far, power, wave, low, midb, row_pad, sem):
    _, core = place_of(tiles)
    rim = pl.ds(pl.multiple_of((1 - core) * TW, HALF), HALF)
    moves = (
        (obj, wave.at[:, :OH, pl.ds(pl.multiple_of(core * HALF, HALF), TW)]),
        (beside, wave.at[:, :OH, rim]),
    )
    copies = [pltpu.make_async_copy(src, dst, sem.at[i]) for i, (src, dst) in enumerate(moves)]
    for copy in copies:
        copy.start()

    row_pad[...] = jnp.zeros_like(row_pad)
    row_pad[0:2, 0 : 2 * BAND + 1] = taps_ref[...]

    def band(part):
        line = jnp.broadcast_to(row_pad[part : part + 1, :], (P_SIZE, 2 * P_SIZE))
        turned = pltpu.roll(line, 2 * P_SIZE - BAND, 1, stride=1, stride_axis=0)
        return turned[:, :P_SIZE]

    band_re = band(0)
    band_im = band(1)
    turned_re = band_re.T
    turned_im = band_im.T
    for which, blocks in enumerate(((band_re, -band_im, band_im), (turned_re, turned_im, -turned_im))):
        stacks[which, :P_SIZE, :P_SIZE] = blocks[0].astype(BF16)
        stacks[which, :P_SIZE, P_SIZE:] = blocks[1].astype(BF16)
        stacks[which, P_SIZE:, :P_SIZE] = blocks[2].astype(BF16)
        stacks[which, P_SIZE:, P_SIZE:] = blocks[0].astype(BF16)
        for half in range(2):
            rows = slice(half * BAND, half * BAND + REACH)
            part = slice(half * HALF, (half + 1) * HALF)
            left[which, half, :REACH, :HALF] = blocks[0][rows, part].astype(BF16)
            left[which, half, :REACH, HALF:] = blocks[1][rows, part].astype(BF16)
            left[which, half, REACH:, :HALF] = blocks[2][rows, part].astype(BF16)
            left[which, half, REACH:, HALF:] = blocks[0][rows, part].astype(BF16)

    for copy in copies:
        copy.wait()

    @pl.loop(0, 3)
    def _(slot):
        here, top_row, offset = window_of(pos_ref, tiles, slot)

        @pl.when(here)
        def _():
            base, extra = aligned(top_row)
            for part in range(2):
                rows = wave[part, pl.ds(base, TALL), :]
                turned = pltpu.roll(rows, lax.rem(EXT - offset, EXT), 1)[:, :P_SIZE]
                patch[slot, part] = pltpu.roll(turned, lax.rem(TALL - extra, TALL), 0)[:P_SIZE]
            power[slot] = jnp.zeros((P_SIZE, P_SIZE), F32)
            sides = (patch.at[slot, 0], patch.at[slot, 1])
            forward(mine, range(GROUP), *sides, left, stacks, low.at[0], midb.at[0], far.at[slot], power.at[slot])


def second_kernel(
    tiles, pos_ref, inten, inward, mine, theirs, far, patch, power, left, stacks, mid_out, rim_out, weight,
    total, meas, far_too, low, midb, ratio, acc,
):
    _, core = place_of(tiles)
    total[...] = jnp.zeros_like(total)
    meas[0] = theirs[MODES]
    meas[1] = inten[core]
    meas[2] = inward[core]
    weight[...] = jnp.zeros_like(weight)

    @pl.loop(0, MODES)
    def _(plane):
        weight[...] += mine[plane] * mine[plane] + theirs[plane] * theirs[plane]

    @pl.loop(0, 3)
    def _(slot):
        here, top_row, offset = window_of(pos_ref, tiles, slot)

        @pl.when(here)
        def _():
            base, extra = aligned(top_row)
            ratio[...] = power[slot]
            sides = (patch.at[slot, 0], patch.at[slot, 1])
            forward(theirs, range(GROUP), *sides, left, stacks, low.at[0], midb.at[0], far_too, ratio)
            ratio[...] = jnp.sqrt(meas[slot]) / jnp.sqrt(ratio[...] + 1.0)
            acc[0] = -weight[...] * patch[slot, 0]
            acc[1] = -weight[...] * patch[slot, 1]
            fields = [(far.at[slot, i], mine, i) for i in range(HELD)]
            fields += [(far_too.at[i], theirs, i) for i in range(HELD)]
            for start in range(0, MODES, GROUP):
                group = fields[start : start + GROUP]
                turn = start // GROUP % 2
                for unit, (source, _, _) in enumerate(group):
                    scaled = ratio[...]
                    put_split(low.at[turn], columns_of(unit), source[:, :P_SIZE] * scaled, source[:, P_SIZE:] * scaled)
                out = mix(left.at[1], stacks[0], low.at[turn], midb.at[turn])
                term_re = 0.0
                term_im = 0.0
                for unit, (_, probe, mode) in enumerate(group):
                    back_re = out[columns_of(unit), :P_SIZE]
                    back_im = out[columns_of(unit), P_SIZE:]
                    pr = probe[2 * mode]
                    pi = probe[2 * mode + 1]
                    term_re += pr * back_re + pi * back_im
                    term_im += pr * back_im - pi * back_re
                acc[0] += term_re
                acc[1] += term_im

            for part in range(2):
                total[part, pl.ds(base, TALL), :] += pltpu.roll(lowered(acc[part], extra, EXT), offset, 1)

    mid_out[...] = total[:, :OH, pl.ds(pl.multiple_of(core * HALF, HALF), TW)]
    rim_out[...] = total[:, :OH, pl.ds(pl.multiple_of((1 - core) * TW, HALF), HALF)]


def denom_kernel(tiles, pos_ref, weight, scale, denom):
    tile, _ = place_of(tiles)
    denom[...] = jnp.zeros_like(denom)
    for parity, shifts in ((0, (-2, -1, 0, 1)), (1, (-1, 0, 1, 2))):
        for shift in shifts:
            inside, top_row, column = slot_of(pos_ref, tile, parity, tiles, shift)
            start = column - HALF - tile * TW

            @pl.when(inside & (start > -P_SIZE) & (start < TW))
            def _():
                base, extra = aligned(top_row)
                wide = lowered(weight[...], extra, 2 * P_SIZE)
                turned = pltpu.roll(wide, jnp.where(start < 0, start + 2 * P_SIZE, start), 1)
                denom[pl.ds(base, TALL), :] += turned[:, :TW]

    scale[...] = 1.0 / (denom[:OH] + 0.5)


ANY = pl.BlockSpec(memory_space=pl.ANY)
HBM = pl.BlockSpec(memory_space=pltpu.HBM)
VMEM = pl.BlockSpec(memory_space=pltpu.VMEM)
SMEM = pl.BlockSpec(memory_space=pltpu.SMEM)


def f32(*shape):
    return jax.ShapeDtypeStruct(shape, F32)


def limit(mib):
    return pltpu.CompilerParams(vmem_limit_bytes=mib * 2**20)


def cost(us):
    return pl.CostEstimate(flops=0, bytes_accessed=int(us * 3.5e6), transcendentals=0)


def local(intensity, positions, object_field, probe_modes, kernel_taps):
    tiles = lax.axis_size("tile")
    modes = lax.axis_size("mode")
    core = lax.rem(lax.axis_index("mode"), 2)
    spots = positions.T

    def along_x(array, flip):
        return lax.ppermute(array, "mode", [(i, i ^ (2 * flip)) for i in range(modes)])

    def swap(array):
        return lax.ppermute(array, "mode", [(i, i ^ 1) for i in range(modes)])

    def from_tile(array, step):
        pairs = []
        for tile in range(tiles):
            for mode in range(modes):
                source = tile + step if mode % 2 == 0 else tile - step
                if 0 <= source < tiles:
                    pairs.append((source * modes + mode, tile * modes + mode))
        return lax.ppermute(array, ("tile", "mode"), pairs)

    ring = [along_x(probe_modes, flip) for flip in (2, 3, 1)]
    edge, held = pl.pallas_call(
        pack_kernel,
        out_shape=(f32(2, OH, HALF), f32(MODES + 1, P_SIZE, P_SIZE)),
        in_specs=[ANY, ANY],
        out_specs=(VMEM, VMEM),
        scratch_shapes=[pltpu.SemaphoreType.DMA((2,))],
        compiler_params=limit(4),
        cost_estimate=cost(2.2),
        name="pack",
    )(object_field, probe_modes)
    beside = from_tile(edge, 1)
    inward = from_tile(intensity, 1)

    def stages(units):
        return [
            pltpu.VMEM((2, 2 * P_SIZE, units * P_SIZE), BF16),
            pltpu.VMEM((2, units * P_SIZE, 2 * P_SIZE), BF16),
        ]

    mine = pl.pallas_call(
        merge_kernel,
        out_shape=f32(MODES + 1, P_SIZE, P_SIZE),
        in_specs=[ANY] * 4,
        out_specs=ANY,
        scratch_shapes=[pltpu.SemaphoreType.DMA((3,))],
        input_output_aliases={0: 0},
        compiler_params=limit(4),
        cost_estimate=cost(1.0),
        name="merge",
    )(held, *ring)
    mine = pl.pallas_call(
        append_kernel,
        out_shape=f32(MODES + 1, P_SIZE, P_SIZE),
        in_specs=[ANY, ANY],
        out_specs=ANY,
        scratch_shapes=[pltpu.SemaphoreType.DMA((1,))],
        input_output_aliases={1: 0},
        compiler_params=limit(4),
        name="append",
    )(inward, mine)
    mine, beside = lax.optimization_barrier((mine, beside))
    theirs = swap(mine)

    patch, left, stacks, far, power = pl.pallas_call(
        functools.partial(first_kernel, tiles),
        out_shape=(
            f32(3, 2, P_SIZE, P_SIZE),
            jax.ShapeDtypeStruct((2, 2, 2 * REACH, 2 * HALF), BF16),
            jax.ShapeDtypeStruct((2, 2 * P_SIZE, 2 * P_SIZE), BF16),
            f32(3, HELD, P_SIZE, 2 * P_SIZE),
            f32(3, P_SIZE, P_SIZE),
        ),
        in_specs=[SMEM, VMEM, ANY, ANY, VMEM],
        out_specs=(VMEM,) * 5,
        scratch_shapes=[pltpu.VMEM((2, OH + 8, EXT), F32)]
        + stages(GROUP)
        + [pltpu.VMEM((8, 2 * P_SIZE), F32), pltpu.SemaphoreType.DMA((2,))],
        compiler_params=limit(16),
        cost_estimate=cost(6.0),
        name="far_of_own_modes",
    )(spots, kernel_taps, object_field, beside, mine)

    middle, rim, weight = pl.pallas_call(
        functools.partial(second_kernel, tiles),
        out_shape=(f32(2, OH, TW), f32(2, OH, HALF), f32(P_SIZE, P_SIZE)),
        in_specs=[SMEM] + [VMEM] * 9,
        out_specs=(VMEM,) * 3,
        scratch_shapes=[
            pltpu.VMEM((2, OH + 8, EXT), F32),
            pltpu.VMEM((3, P_SIZE, P_SIZE), F32),
            pltpu.VMEM((HELD, P_SIZE, 2 * P_SIZE), F32),
        ]
        + stages(GROUP)
        + [pltpu.VMEM((P_SIZE, P_SIZE), F32), pltpu.VMEM((2, P_SIZE, P_SIZE), F32)],
        compiler_params=limit(20),
        cost_estimate=cost(10.0),
        name="update_terms",
    )(spots, intensity, inward, mine, theirs, far, patch, power, left, stacks)

    arrived = from_tile(rim, -1)
    scale = pl.pallas_call(
        functools.partial(denom_kernel, tiles),
        out_shape=f32(OH, TW),
        in_specs=[SMEM, VMEM],
        out_specs=VMEM,
        scratch_shapes=[pltpu.VMEM((OH + 8, TW), F32)],
        compiler_params=limit(4),
        cost_estimate=cost(3.5),
        name="denominator",
    )(spots, weight)
    blank = jnp.zeros_like(arrived)
    low = jnp.where(core == 0, arrived, blank)
    high = jnp.where(core == 0, blank, arrived)
    terms = (middle + jnp.concatenate([low, high], axis=2)) * scale
    return object_field + (terms + swap(terms))


def solution(mesh):
    return jax.shard_map(
        local,
        mesh=mesh,
        in_specs=(
            P("tile", None, None),
            P(),
            P(None, None, "tile"),
            P("mode", None, None, None),
            P(),
        ),
        out_specs=P(None, None, "tile"),
        check_vma=False,
    )
```
